256 devices in a mesh: ctx: 128 (over z, x, y_hi, core), head: 2 (over y_lo).
Axes of the slice: x: 4, y: 4 (y_hi: 2, y_lo: 2; y = y_hi * 2 + y_lo), z: 8, core: 2. Of those that a mesh axis runs over, the one named last changes fastest.
Arguments:
- fw_q: bfloat16 [32768, 2048], P('ctx', 'head'), may hold values from -6 to 6
- fw_k: bfloat16 [32768, 2048], P('ctx', 'head'), may hold values from -16 to 16
- fw_v: bfloat16 [32768, 2048], P('ctx', 'head'), may hold values from -6 to 6
- fw_lr: float32 [32768, 4], P('ctx', 'head'), may hold values from 0.1 to 3
- fast_gate: bfloat16 [4, 512, 512], P('head'), may hold values from -0.25 to 0.25
- fast_up: bfloat16 [4, 512, 512], P('head'), may hold values from -0.25 to 0.25
- fast_down: bfloat16 [4, 512, 512], P('head'), may hold values from -0.25 to 0.25
- attn_q: bfloat16 [32768, 2048], P('ctx', 'head'), may hold values from -96 to 96
- attn_k: bfloat16 [32768, 2048], P('ctx', 'head'), may hold values from -10 to 10
- attn_v: bfloat16 [32768, 2048], P('ctx', 'head'), may hold values from -6 to 6
Outputs:
- mixed_out: bfloat16 [32768, 2048], P(('ctx', 'head'))
The draws below stay inside these ranges and needn't reach their ends.
All inputs are finite; a program needn't handle non-finite values.
Results may differ from the reference program's by a relative error of at most 0.0095.
Values may be sent and summed in bfloat16 or wider, within the bound.
No kernel may reach another device: no remote copies, remote signals or barrier semaphores. Data moves between devices by JAX's collectives and lax.ppermute only.
A program may use at most 128 MiB of HBM per device.

```python
import math
import jax
import jax.numpy as jnp
from jax import lax

DH = 512
FW_HEADS = 4
SWA_DH = 128
WINDOW = 128
NS_ITERS = 2
D = 2048
SWA_HEADS = 16
TOKENS = 32768


def draw_fw_k(key, part):
    key_scale, key_base = jax.random.split(jax.random.fold_in(key, 11), 2)
    scales = jnp.exp(jax.random.uniform(key_scale, (D,), jnp.float32, 0.0, math.log(10.0)))
    scales = scales / jnp.sqrt(jnp.mean(scales * scales))
    base = jnp.clip(jax.random.normal(key_base, (TOKENS, D), jnp.float32), -6.0, 6.0)
    return (base * scales[None, :]).astype(jnp.bfloat16)


def draw_fw_lr(key, part):
    ramp = 1.0 + 2.0 * jnp.arange(TOKENS, dtype=jnp.float32)[:, None] / (TOKENS - 1)
    base = jnp.exp(jax.random.uniform(jax.random.fold_in(key, 13), (TOKENS, FW_HEADS), jnp.float32, math.log(0.1), 0.0))
    return base * ramp


def attention_pair(key):
    key_q, key_k = jax.random.split(jax.random.fold_in(key, 23), 2)
    queries = 1.5 * jnp.clip(jax.random.normal(key_q, (TOKENS, D), jnp.float32), -6.0, 6.0)
    key_rows = 1.5 * jnp.clip(jax.random.normal(key_k, (TOKENS, D), jnp.float32), -6.0, 6.0)
    return (queries, key_rows)


def draw_attn_q(key, part):
    return attention_pair(key)[0].astype(jnp.bfloat16)


def draw_attn_k(key, part):
    return attention_pair(key)[1].astype(jnp.bfloat16)


def block_levels(stream_key, shape, cuts, smallest, largest):
    level = 1.0
    for dim, parts in cuts:
        draws = jax.random.uniform(jax.random.fold_in(jax.random.fold_in(stream_key, 6), dim), (parts,), jnp.float32, smallest / len(cuts), largest / len(cuts))
        level = level * jnp.repeat(jnp.exp(draws), shape[dim] // parts).reshape((-1,) + (1,) * (len(shape) - 1 - dim))
    return level


def centred(rng, shape, width, bound, cuts=(), kind=jnp.bfloat16):
    entries = width * jax.random.normal(rng, shape, jnp.float32)
    if cuts:
        entries = entries * block_levels(rng, shape, cuts, -0.22, 0.18)
    return jnp.clip(entries, -bound, bound).astype(kind)


def setup_inputs(seed: int = 0) -> dict:
    key_list = jax.random.split(jax.random.key(seed), 11)
    fw_q = centred(key_list[0], (TOKENS, D), 1.0, 6.0, ((0, 128), (1, 2)))
    fw_k = draw_fw_k(jax.random.fold_in(key_list[10], 71), 0)
    fw_v = centred(key_list[2], (TOKENS, D), 1.0, 6.0, ((0, 128), (1, 2)))
    fw_lr = draw_fw_lr(jax.random.fold_in(key_list[10], 71), 0)
    fast_gate = centred(key_list[4], (FW_HEADS, DH, DH), DH ** -0.5, 0.25, ((0, 2),))
    fast_up = centred(key_list[5], (FW_HEADS, DH, DH), DH ** -0.5, 0.25, ((0, 2),))
    fast_down = centred(key_list[6], (FW_HEADS, DH, DH), DH ** -0.5, 0.25, ((0, 2),))
    attn_q = draw_attn_q(jax.random.fold_in(key_list[10], 71), 0)
    attn_k = draw_attn_k(jax.random.fold_in(key_list[10], 71), 0)
    attn_v = centred(key_list[9], (TOKENS, D), 1.0, 6.0, ((0, 128), (1, 2)))
    return {"fw_q": fw_q, "fw_k": fw_k, "fw_v": fw_v, "fw_lr": fw_lr, "fast_gate": fast_gate, "fast_up": fast_up, "fast_down": fast_down, "attn_q": attn_q, "attn_k": attn_k, "attn_v": attn_v}


linear_coef = 3.4445
square_coef = -4.775
quartic_coef = 2.0315
epsilon = 1e-06

def mat_prod(left, right):
    return jnp.dot(left, right, preferred_element_type=jnp.float32)

def head_gradients(key_rows, value_rows, rates, gate_weight, up_weight, down_weight):
    pre_gate = mat_prod(key_rows, gate_weight)
    pre_up = mat_prod(key_rows, up_weight)
    sigmoid_gate = jax.nn.sigmoid(pre_gate)
    activated = pre_gate * sigmoid_gate
    hidden = (activated * pre_up).astype(jnp.bfloat16)
    out_grad = (-(rates[:, None] * value_rows.astype(jnp.float32))).astype(jnp.bfloat16)
    grad_down = mat_prod(hidden.T, out_grad)
    hidden_grad = mat_prod(out_grad, down_weight.T)
    slope = sigmoid_gate * (1.0 + pre_gate * (1.0 - sigmoid_gate))
    gate_grad = (hidden_grad * pre_up * slope).astype(jnp.bfloat16)
    up_grad = (hidden_grad * activated).astype(jnp.bfloat16)
    grad_gate = mat_prod(key_rows.T, gate_grad)
    grad_up = mat_prod(key_rows.T, up_grad)
    return (grad_gate, grad_up, grad_down)

def orthogonalize(gradient):
    iterate = (gradient / jnp.sqrt(jnp.sum(gradient * gradient) + epsilon)).astype(jnp.bfloat16)
    for sweep_index in range(NS_ITERS):
        gram_matrix = mat_prod(iterate, iterate.T).astype(jnp.bfloat16)
        square = mat_prod(gram_matrix, gram_matrix)
        polynomial = (square_coef * gram_matrix.astype(jnp.float32) + quartic_coef * square).astype(jnp.bfloat16)
        iterate = (linear_coef * iterate.astype(jnp.float32) + mat_prod(polynomial, iterate)).astype(jnp.bfloat16)
    return iterate

def refresh(weight, update):
    initial = weight.astype(jnp.float32)
    stepped = initial - update.astype(jnp.float32)
    old_norm = jnp.sqrt(lax.optimization_barrier(jnp.sum(initial * initial, axis=-2, keepdims=True)) + epsilon)
    new_norm = jnp.sqrt(lax.optimization_barrier(jnp.sum(stepped * stepped, axis=-2, keepdims=True)) + epsilon)
    return (stepped * (old_norm / new_norm)).astype(jnp.bfloat16)

def answer(queries, gate_weight, up_weight, down_weight):
    pre_gate = mat_prod(queries, gate_weight)
    pre_up = mat_prod(queries, up_weight)
    query_hidden = (jax.nn.silu(pre_gate) * pre_up).astype(jnp.bfloat16)
    return mat_prod(query_hidden, down_weight)

def window_attention(queries, key_rows, value_rows):
    blocks = TOKENS // WINDOW
    padding = jnp.zeros((WINDOW, D), jnp.bfloat16)
    keys_padded = jnp.concatenate([padding, key_rows], axis=0)
    values_padded = jnp.concatenate([padding, value_rows], axis=0)
    score_scale = 1.0 / math.sqrt(SWA_DH)

    def one_block(block_index):
        offset = block_index * WINDOW
        query_blk = lax.dynamic_slice_in_dim(queries, offset, WINDOW, 0).astype(jnp.float32).reshape(WINDOW, SWA_HEADS, SWA_DH)
        key_blk = lax.dynamic_slice_in_dim(keys_padded, offset, 2 * WINDOW, 0).astype(jnp.float32).reshape(2 * WINDOW, SWA_HEADS, SWA_DH)
        value_blk = lax.dynamic_slice_in_dim(values_padded, offset, 2 * WINDOW, 0).astype(jnp.float32).reshape(2 * WINDOW, SWA_HEADS, SWA_DH)
        scores = jnp.einsum('qhd,khd->hqk', query_blk, key_blk) * score_scale
        query_pos = offset + jnp.arange(WINDOW, dtype=jnp.int32)
        key_pos = offset - WINDOW + jnp.arange(2 * WINDOW, dtype=jnp.int32)
        allowed = (key_pos[None, :] <= query_pos[:, None]) & (key_pos[None, :] > query_pos[:, None] - WINDOW) & (key_pos[None, :] >= 0)
        masked = jnp.where(allowed[None, :, :], scores, -jnp.inf)
        row_peak = lax.optimization_barrier(jnp.max(masked, axis=-1, keepdims=True))
        exponent = jnp.exp(masked - row_peak)
        row_total = lax.optimization_barrier(jnp.sum(exponent, axis=-1, keepdims=True))
        weights_bf = (exponent / row_total).astype(jnp.bfloat16)
        result = jnp.einsum('hqk,khd->qhd', weights_bf.astype(jnp.float32), value_blk)
        return result.reshape(WINDOW, D)
    return lax.map(one_block, jnp.arange(blocks, dtype=jnp.int32)).reshape(TOKENS, D)

def reference(fw_q, fw_k, fw_v, fw_lr, fast_gate, fast_up, fast_down, attn_q, attn_k, attn_v):
    pieces = []
    for head_index in range(FW_HEADS):
        offset = head_index * DH
        gradients = head_gradients(fw_k[:, offset:offset + DH], fw_v[:, offset:offset + DH], fw_lr[:, head_index], fast_gate[head_index], fast_up[head_index], fast_down[head_index])
        weights = (fast_gate[head_index], fast_up[head_index], fast_down[head_index])
        renewed = [refresh(weights[matrix_index], orthogonalize(gradients[matrix_index])) for matrix_index in range(3)]
        pieces.append(answer(fw_q[:, offset:offset + DH], renewed[0], renewed[1], renewed[2]).astype(jnp.bfloat16))
    memory = jnp.concatenate(pieces, axis=1)
    attended = window_attention(attn_q, attn_k, attn_v)
    return (memory.astype(jnp.float32) + attended).astype(jnp.bfloat16)
```

```python
import math

import jax
import jax.numpy as jnp
from jax import lax
from jax.sharding import Mesh, PartitionSpec as P

SWA_DH = 128
WINDOW = 128
NS_ITERS = 2
DH = 512

linear_coef = 3.4445
square_coef = -4.775
quartic_coef = 2.0315
epsilon = 1e-06

CHIPS = ("z", "x", "yh")
PLANE = ("x", "yh")
QUAD = ("core", "yl")


def mat(left, right, dims):
    return lax.dot_general(left, right, (dims, ((), ())), preferred_element_type=jnp.float32)


def refresh(weight, update):
    initial = weight.astype(jnp.float32)
    stepped = initial - update.astype(jnp.float32)
    old_norm = jnp.sqrt(jnp.sum(initial * initial, axis=-2, keepdims=True) + epsilon)
    new_norm = jnp.sqrt(jnp.sum(stepped * stepped, axis=-2, keepdims=True) + epsilon)
    return (stepped * (old_norm / new_norm)).astype(jnp.bfloat16)


def core_exchange(arrays):
    rows = arrays[0].shape[0]
    packed = jnp.stack([a.reshape(rows, 2, DH).transpose(1, 0, 2) for a in arrays], axis=1)
    moved = lax.all_to_all(packed, "core", split_axis=0, concat_axis=0, tiled=True)
    return [moved[:, i].reshape(2 * rows, DH) for i in range(len(arrays))]


def attend(q, k, v, halo, first):
    blocks = q.shape[0] // WINDOW
    heads = q.shape[1] // SWA_DH

    def split(a):
        return a.reshape(-1, WINDOW, heads, SWA_DH)

    keys = split(jnp.concatenate([halo[0], k], axis=0))
    values = split(jnp.concatenate([halo[1], v], axis=0))
    q = split(q)
    scale = 1.0 / math.sqrt(SWA_DH)

    def scores(keys):
        return jnp.einsum("bqhd,bkhd->bhqk", q, keys, preferred_element_type=jnp.float32) * scale

    i = jnp.arange(WINDOW, dtype=jnp.int32)
    older = i[None, :] > i[:, None]
    block = jnp.arange(blocks, dtype=jnp.int32)[:, None, None, None]
    old_scores = jnp.where(older & ((block > 0) | jnp.logical_not(first)), scores(keys[:-1]), -jnp.inf)
    new_scores = jnp.where(jnp.logical_not(older), scores(keys[1:]), -jnp.inf)
    both = jnp.concatenate([old_scores, new_scores], axis=-1)
    peak = jnp.max(both, axis=-1, keepdims=True)
    exponent = jnp.exp(both - peak)
    total = jnp.sum(exponent, axis=-1, keepdims=True)
    probs = (exponent / total).astype(jnp.bfloat16)
    window_values = jnp.concatenate([values[:-1], values[1:]], axis=1)
    result = jnp.einsum("bhqk,bkhd->bqhd", probs, window_values, preferred_element_type=jnp.float32)
    return result.reshape(blocks * WINDOW, heads * SWA_DH)


def shards(fw_q, fw_k, fw_v, fw_lr, fast_gate, fast_up, fast_down, attn_q, attn_k, attn_v):
    rows = fw_k.shape[0]
    core = lax.axis_index("core")
    chip = lax.axis_index(CHIPS)
    gate, up, down = (
        lax.dynamic_index_in_dim(w, core, 0, keepdims=False) for w in (fast_gate, fast_up, fast_down)
    )
    rates = jnp.repeat(fw_lr, DH, axis=1)
    out_grad = (-(rates * fw_v.astype(jnp.float32))).astype(jnp.bfloat16)
    keys, out_grad = core_exchange([fw_k, out_grad])
    nn, nt, tn = ((1,), (0,)), ((1,), (1,)), ((0,), (0,))
    pre_gate = mat(keys, gate, nn)
    pre_up = mat(keys, up, nn)
    sigmoid_gate = jax.nn.sigmoid(pre_gate)
    activated = pre_gate * sigmoid_gate
    hidden = (activated * pre_up).astype(jnp.bfloat16)
    grad_down = mat(hidden, out_grad, tn)
    hidden_grad = mat(out_grad, down, nt)
    slope = sigmoid_gate * (1.0 + pre_gate * (1.0 - sigmoid_gate))
    gate_grad = (hidden_grad * pre_up * slope).astype(jnp.bfloat16)
    up_grad = (hidden_grad * activated).astype(jnp.bfloat16)
    grad_gate = mat(keys, gate_grad, tn)
    grad_up = mat(keys, up_grad, tn)
    partial = jnp.concatenate(
        [g.astype(jnp.bfloat16) for g in (grad_gate, grad_up, grad_down)], axis=0
    )
    plane = lax.axis_size(PLANE)
    depth = lax.axis_size("z")
    part = partial.reshape(plane, -1, DH)
    part = lax.all_to_all(part, PLANE, split_axis=0, concat_axis=0, tiled=True)
    part = jnp.sum(part.astype(jnp.float32), axis=0).astype(jnp.bfloat16).reshape(depth, -1, DH)
    part = lax.all_to_all(part, "z", split_axis=0, concat_axis=0, tiled=True)
    part = jnp.sum(part.astype(jnp.float32), axis=0).astype(jnp.bfloat16)
    part = lax.all_to_all(
        jnp.broadcast_to(part, (depth,) + part.shape), "z", split_axis=0, concat_axis=0, tiled=True
    ).reshape(-1, DH)
    summed = lax.all_to_all(
        jnp.broadcast_to(part, (plane,) + part.shape), PLANE, split_axis=0, concat_axis=0, tiled=True
    ).reshape(3, DH, DH)

    queries, q, k, v = core_exchange([fw_q, attn_q, attn_k, attn_v])
    chips = lax.axis_size(CHIPS)
    halo = lax.ppermute(
        jnp.stack([k[-WINDOW:], v[-WINDOW:]]), CHIPS, [(s, s + 1) for s in range(chips - 1)]
    )
    attended = attend(q, k, v, halo, chip == 0)

    summed = summed.astype(jnp.float32)
    norm_total = jnp.sum(summed * summed, axis=(1, 2), keepdims=True)
    iterate = (summed / jnp.sqrt(norm_total + epsilon)).astype(jnp.bfloat16)
    for _ in range(NS_ITERS):
        gram = jnp.einsum(
            "bij,bkj->bik", iterate, iterate, preferred_element_type=jnp.float32
        ).astype(jnp.bfloat16)
        square = jnp.einsum("bij,bjk->bik", gram, gram, preferred_element_type=jnp.float32)
        polynomial = (square_coef * gram.astype(jnp.float32) + quartic_coef * square).astype(
            jnp.bfloat16
        )
        iterate = (
            linear_coef * iterate.astype(jnp.float32)
            + jnp.einsum("bij,bjk->bik", polynomial, iterate, preferred_element_type=jnp.float32)
        ).astype(jnp.bfloat16)
    renewed = refresh(jnp.stack([gate, up, down]), iterate)
    query_gate = mat(queries, renewed[0], nn)
    query_up = mat(queries, renewed[1], nn)
    query_hidden = (jax.nn.silu(query_gate) * query_up).astype(jnp.bfloat16)
    memory = mat(query_hidden, renewed[2], nn).astype(jnp.bfloat16)
    mixed = (memory.astype(jnp.float32) + attended).astype(jnp.bfloat16)
    moved = lax.all_to_all(
        mixed.reshape(4, -1, DH), QUAD, split_axis=0, concat_axis=0, tiled=True
    )
    moved = moved.reshape(2, 2, -1, DH).transpose(2, 1, 0, 3)
    return moved.reshape(2 * rows // 4, 4 * DH)


def solution(mesh):
    fine = Mesh(mesh.devices.reshape(8, 4, 2, 2, 2), ("z", "x", "yh", "core", "yl"))
    ctx = ("z", "x", "yh", "core")
    wide = P(ctx, "yl")
    weight = P("yl", None, None)
    in_specs = (wide, wide, wide, wide, weight, weight, weight, wide, wide, wide)
    out_specs = P(ctx + ("yl",), None)
    return jax.shard_map(shards, mesh=fine, in_specs=in_specs, out_specs=out_specs, check_vma=False)
```

```python
import math

import jax
import jax.numpy as jnp
from jax import lax
from jax.experimental import pallas as pl
from jax.experimental.pallas import tpu as pltpu
from jax.sharding import Mesh, PartitionSpec as P

SWA_DH = 128
WINDOW = 128
NS_ITERS = 2
DH = 512
HALF = 256

linear_coef = 3.4445
square_coef = -4.775
quartic_coef = 2.0315
epsilon = 1e-06

CHIPS = ("z", "x", "yh")
PLANE = ("x", "yh")
QUAD = ("core", "yl")

BF = jnp.bfloat16
F32 = jnp.float32
NN, NT, TN = ((1,), (0,)), ((1,), (1,)), ((0,), (0,))


def mat(left, right, dims):
    return lax.dot_general(left, right, (dims, ((), ())), preferred_element_type=F32)


def shape(dims, dtype=BF):
    return jax.ShapeDtypeStruct(dims, dtype)


def cost(flops, nbytes, trans=0):
    return pl.CostEstimate(flops=flops, bytes_accessed=nbytes, transcendentals=trans)


def pack_grad_body(k_ref, v_ref, lr_ref, out_ref):
    head = pl.program_id(0)
    rows = k_ref.shape[0]
    rates = jnp.where(head == 0, lr_ref[0:1, :], lr_ref[1:2, :])
    rates = jnp.broadcast_to(rates, (SWA_DH, rows)).T
    out_ref[0, 0] = k_ref[...]
    for j in range(0, DH, SWA_DH):
        cols = slice(j, j + SWA_DH)
        out_ref[0, 1, :, cols] = (-(rates * v_ref[:, cols].astype(F32))).astype(BF)


def pack_grad(fw_k, fw_v, fw_lr):
    rows = fw_k.shape[0]
    wide = pl.BlockSpec((rows, DH), lambda h: (0, h))
    return pl.pallas_call(
        pack_grad_body,
        grid=(2,),
        in_specs=[wide, wide, pl.BlockSpec((2, rows), lambda h: (0, 0))],
        out_specs=pl.BlockSpec((1, 2, rows, DH), lambda h: (h, 0, 0, 0)),
        out_shape=shape((2, 2, rows, DH)),
        cost_estimate=cost(rows * 1024, 8 * rows * 1024),
        name="pack_grad",
    )(fw_k, fw_v, fw_lr.T)


def pack_rest_body(a_ref, b_ref, c_ref, d_ref, out_ref):
    for i, ref in enumerate((a_ref, b_ref, c_ref, d_ref)):
        out_ref[0, i] = ref[...]


def pack_rest(arrays):
    rows = arrays[0].shape[0]
    wide = pl.BlockSpec((rows, DH), lambda h: (0, h))
    return pl.pallas_call(
        pack_rest_body,
        grid=(2,),
        in_specs=[wide] * 4,
        out_specs=pl.BlockSpec((1, 4, rows, DH), lambda h: (h, 0, 0, 0)),
        out_shape=shape((2, 4, rows, DH)),
        cost_estimate=cost(0, 16 * rows * 1024),
        name="pack_rest",
    )(*arrays)


def grads_body(core_ref, moved_ref, gate_ref, up_ref, down_ref, out_ref):
    del core_ref
    half = pl.program_id(0)
    keys = moved_ref[:, 0].reshape(-1, DH)
    out_grad = moved_ref[:, 1].reshape(-1, DH)
    pre_gate = mat(keys, gate_ref[0], NN)
    pre_up = mat(keys, up_ref[0], NN)
    hidden_grad = mat(out_grad, down_ref[0], NT)
    sigmoid_gate = jax.nn.sigmoid(pre_gate)
    activated = pre_gate * sigmoid_gate
    hidden = (activated * pre_up).astype(BF)
    slope = sigmoid_gate * (1.0 + pre_gate * (1.0 - sigmoid_gate))
    gate_grad = (hidden_grad * pre_up * slope).astype(BF)
    up_grad = (hidden_grad * activated).astype(BF)
    grad_gate = mat(keys, gate_grad, TN).astype(BF)
    grad_up = mat(keys, up_grad, TN).astype(BF)
    grad_down = mat(hidden, out_grad, TN).astype(BF)
    for h in range(2):

        @pl.when(half == h)
        def _():
            cols = slice(h * HALF, (h + 1) * HALF)
            out_ref[0, :, cols] = grad_gate
            out_ref[1, :, cols] = grad_up
            out_ref[2, cols, :] = grad_down


def grads(core, moved, gate, up, down):
    tokens = moved.shape[0] * moved.shape[2]
    wide = pl.BlockSpec((1, DH, HALF), lambda h, c: (c[0], 0, h))
    return pl.pallas_call(
        grads_body,
        grid_spec=pltpu.PrefetchScalarGridSpec(
            num_scalar_prefetch=1,
            grid=(2,),
            in_specs=[
                pl.BlockSpec(moved.shape, lambda h, c: (0, 0, 0, 0)),
                wide,
                wide,
                pl.BlockSpec((1, HALF, DH), lambda h, c: (c[0], h, 0)),
            ],
            out_specs=pl.BlockSpec((3, DH, DH), lambda h, c: (0, 0, 0)),
        ),
        out_shape=shape((3, DH, DH)),
        cost_estimate=cost(12 * tokens * DH * DH, 8 * DH * DH * 2, tokens * DH),
        name="grads",
    )(core, moved, gate, up, down)


def sum_body(in_ref, out_ref):
    total = in_ref[0].astype(F32)
    for i in range(1, in_ref.shape[0]):
        total += in_ref[i].astype(F32)
    out_ref[...] = total.astype(BF)


def summed(parts, steps):
    count, rows, cols = parts.shape
    return pl.pallas_call(
        sum_body,
        grid=(steps,),
        in_specs=[pl.BlockSpec((count, rows // steps, cols), lambda i: (0, i, 0))],
        out_specs=pl.BlockSpec((rows // steps, cols), lambda i: (i, 0)),
        out_shape=shape((rows, cols)),
        cost_estimate=cost(count * rows * cols, 2 * count * rows * cols),
        name="plane_sum",
    )(parts)


def sum_spread_body(in_ref, out_ref):
    total = in_ref[0].astype(F32)
    for i in range(1, in_ref.shape[0]):
        total += in_ref[i].astype(F32)
    total = total.astype(BF)
    for i in range(out_ref.shape[0]):
        out_ref[i] = total


def sum_spread(parts):
    return pl.pallas_call(
        sum_spread_body,
        out_shape=shape(parts.shape),
        cost_estimate=cost(parts.size, 4 * parts.size),
        name="depth_sum",
    )(parts)


def spread_body(in_ref, out_ref, sems):
    copies = [
        pltpu.make_async_copy(in_ref, out_ref.at[i], sems.at[i]) for i in range(out_ref.shape[0])
    ]
    for copy in copies:
        copy.start()
    for copy in copies:
        copy.wait()


def spread(part, count):
    return pl.pallas_call(
        spread_body,
        in_specs=[pl.BlockSpec(memory_space=pltpu.VMEM)],
        out_specs=pl.BlockSpec(memory_space=pl.ANY),
        out_shape=shape((count,) + part.shape),
        scratch_shapes=[pltpu.SemaphoreType.DMA((count,))],
        cost_estimate=cost(0, 2 * (count + 1) * part.size),
        name="spread",
    )(part)


def attend_body(chip_ref, q_ref, k_ref, v_ref, halo_ref, out_ref):
    scale = 1.0 / math.sqrt(SWA_DH)
    row = lax.broadcasted_iota(jnp.int32, (WINDOW, WINDOW), 0)
    col = lax.broadcasted_iota(jnp.int32, (WINDOW, WINDOW), 1)
    older = col > row
    keys = k_ref[:, 0].reshape(-1, SWA_DH)
    values = v_ref[:, 0].reshape(-1, SWA_DH)
    queries = q_ref[:, 0].reshape(-1, SWA_DH)
    old_keys, old_values = halo_ref[0], halo_ref[1]
    seen = older & (chip_ref[0] > 0)
    for b in range(queries.shape[0] // WINDOW):
        rows = slice(b * WINDOW, (b + 1) * WINDOW)
        q, k, v = queries[rows], keys[rows], values[rows]
        old = jnp.where(seen, mat(q, old_keys, NT) * scale, -jnp.inf)
        new = jnp.where(older, -jnp.inf, mat(q, k, NT) * scale)
        peak = jnp.max(jnp.maximum(old, new), axis=-1, keepdims=True)
        old = jnp.exp(old - peak)
        new = jnp.exp(new - peak)
        total = jnp.sum(old + new, axis=-1, keepdims=True)
        old = (old / total).astype(BF)
        new = (new / total).astype(BF)
        out_ref[rows, :] = mat(old, old_values, NN) + mat(new, v, NN)
        old_keys, old_values, seen = k, v, older


def attend(chip, moved, halo):
    rows = moved.shape[2]
    heads = DH // SWA_DH

    def part(i):
        return pl.BlockSpec((2, 1, rows, SWA_DH), lambda h, c: (0, i, 0, h))

    return pl.pallas_call(
        attend_body,
        grid_spec=pltpu.PrefetchScalarGridSpec(
            num_scalar_prefetch=1,
            grid=(heads,),
            in_specs=[
                part(1),
                part(2),
                part(3),
                pl.BlockSpec((2, WINDOW, SWA_DH), lambda h, c: (0, 0, h)),
            ],
            out_specs=pl.BlockSpec((2 * rows, SWA_DH), lambda h, c: (0, h)),
        ),
        out_shape=shape((2 * rows, DH), F32),
        cost_estimate=cost(2 * rows * 8 * WINDOW * DH, 12 * rows * DH, 4 * rows * DH),
        name="window_attention",
    )(chip, moved, moved, moved, halo)


def refresh(weight, update):
    initial = weight.astype(F32)
    stepped = initial - update.astype(F32)
    old_norm = jnp.sqrt(jnp.sum(initial * initial, axis=0, keepdims=True) + epsilon)
    new_norm = jnp.sqrt(jnp.sum(stepped * stepped, axis=0, keepdims=True) + epsilon)
    return (stepped * (old_norm / new_norm)).astype(BF)


def finish_body(core_ref, sum_ref, gate_ref, up_ref, down_ref, q_ref, att_ref, out_ref):
    del core_ref
    iterates = []
    for m in range(3):
        gradient = sum_ref[m].astype(F32)
        norm_total = jnp.sum(gradient * gradient)
        iterates.append((gradient * (1.0 / jnp.sqrt(norm_total + epsilon))).astype(BF))
    for _ in range(NS_ITERS):
        grams = [mat(x, x, NT).astype(BF) for x in iterates]
        polys = [
            (square_coef * g.astype(F32) + quartic_coef * mat(g, g, NN)).astype(BF) for g in grams
        ]
        iterates = [
            (linear_coef * x.astype(F32) + mat(p, x, NN)).astype(BF)
            for p, x in zip(polys, iterates)
        ]
    renewed = [refresh(w[0], x) for w, x in zip((gate_ref, up_ref, down_ref), iterates)]
    queries = q_ref[:, 0].reshape(-1, DH)
    query_gate = mat(queries, renewed[0], NN)
    query_up = mat(queries, renewed[1], NN)
    query_hidden = (query_gate * jax.nn.sigmoid(query_gate) * query_up).astype(BF)
    memory = mat(query_hidden, renewed[2], NN).astype(BF)
    out_ref[...] = (memory.astype(F32) + att_ref[...]).astype(BF)


def finish(core, total, gate, up, down, moved, attended):
    rows = moved.shape[2]
    weight = pl.BlockSpec((1, DH, DH), lambda i, c: (c[0], 0, 0))
    full = pl.BlockSpec((2 * rows, DH), lambda i, c: (0, 0))
    return pl.pallas_call(
        finish_body,
        grid_spec=pltpu.PrefetchScalarGridSpec(
            num_scalar_prefetch=1,
            grid=(1,),
            in_specs=[
                pl.BlockSpec((3, DH, DH), lambda i, c: (0, 0, 0)),
                weight,
                weight,
                weight,
                pl.BlockSpec((2, 1, rows, DH), lambda i, c: (0, 0, 0, 0)),
                full,
            ],
            out_specs=full,
        ),
        out_shape=shape((2 * rows, DH)),
        cost_estimate=cost(42 * DH**3, 20 * DH * DH, rows * DH),
        name="finish",
    )(core, total, gate, up, down, moved, attended)


def unpack_body(in_ref, out_ref):
    out_ref[...] = in_ref[0]


def unpack(moved):
    count, rows, cols = moved.shape
    return pl.pallas_call(
        unpack_body,
        grid=(count,),
        in_specs=[pl.BlockSpec((1, rows, cols), lambda i: (i, 0, 0))],
        out_specs=pl.BlockSpec((rows, cols), lambda i: (0, (i % 2) * 2 + i // 2)),
        out_shape=shape((rows, count * cols)),
        cost_estimate=cost(0, 4 * moved.size),
        name="unpack",
    )(moved)


def swap(value, axes):
    return lax.all_to_all(value, axes, split_axis=0, concat_axis=0, tiled=True)


def shards(fw_q, fw_k, fw_v, fw_lr, fast_gate, fast_up, fast_down, attn_q, attn_k, attn_v):
    core = lax.axis_index("core").astype(jnp.int32).reshape(1)
    chip = lax.axis_index(CHIPS).astype(jnp.int32).reshape(1)
    moved = swap(pack_grad(fw_k, fw_v, fw_lr), "core")
    partial = grads(core, moved, fast_gate, fast_up, fast_down)
    plane = lax.axis_size(PLANE)
    depth = lax.axis_size("z")
    partial, *rest = lax.optimization_barrier((partial, fw_q, attn_q, attn_k, attn_v))
    part = swap(partial.reshape(plane, -1, DH), PLANE)
    moved = swap(pack_rest(rest), "core")
    part = summed(part, 4)
    part, moved = lax.optimization_barrier((part, moved))
    part = swap(part.reshape(depth, -1, DH), "z")
    chips = lax.axis_size(CHIPS)
    halo = lax.ppermute(moved[1, 2:, -WINDOW:], CHIPS, [(s, s + 1) for s in range(chips - 1)])
    part = swap(sum_spread(part), "z").reshape(-1, DH)
    total = swap(spread(part, plane), PLANE).reshape(3, DH, DH)
    attended = attend(chip, moved, halo)
    mixed = finish(core, total, fast_gate, fast_up, fast_down, moved, attended)
    return unpack(swap(mixed.reshape(4, -1, DH), QUAD))


def solution(mesh):
    fine = Mesh(mesh.devices.reshape(8, 4, 2, 2, 2), ("z", "x", "yh", "core", "yl"))
    ctx = ("z", "x", "yh", "core")
    wide = P(ctx, "yl")
    weight = P("yl", None, None)
    in_specs = (wide, wide, wide, wide, weight, weight, weight, wide, wide, wide)
    out_specs = P(ctx + ("yl",), None)
    return jax.shard_map(shards, mesh=fine, in_specs=in_specs, out_specs=out_specs, check_vma=False)
```

```python
import math

import jax
import jax.numpy as jnp
from jax import lax
from jax.experimental import pallas as pl
from jax.experimental.pallas import tpu as pltpu
from jax.sharding import Mesh, PartitionSpec as P

SWA_DH = 128
WINDOW = 128
NS_ITERS = 2
DH = 512
HALF = 256

linear_coef = 3.4445
square_coef = -4.775
quartic_coef = 2.0315
epsilon = 1e-06


CHIPS = ("z", "x", "yh")
PLANE = ("x", "yh")
QUAD = ("core", "yl")

BF = jnp.bfloat16
F32 = jnp.float32
NN, NT, TN = ((1,), (0,)), ((1,), (1,)), ((0,), (0,))


def mat(left, right, dims):
    return lax.dot_general(left, right, (dims, ((), ())), preferred_element_type=F32)


def shape(dims, dtype=BF):
    return jax.ShapeDtypeStruct(dims, dtype)


def cost(flops, nbytes, trans=0):
    return pl.CostEstimate(flops=flops, bytes_accessed=nbytes, transcendentals=trans)


def vmem(value):
    return pltpu.with_memory_space_constraint(value, pltpu.VMEM)


def hbm(*values):
    return [pltpu.with_memory_space_constraint(v, pltpu.HBM) for v in values]


VM = pl.BlockSpec(memory_space=pltpu.VMEM)
SM = pl.BlockSpec(memory_space=pltpu.SMEM)
PARAMS = pltpu.CompilerParams(vmem_limit_bytes=24 * 1024 * 1024)


def on_chip(dims, dtype=BF):
    return pltpu.VMEM(dims, dtype)


HBM = pl.BlockSpec(memory_space=pltpu.HBM)


def half(ref, which):
    return ref.at[:, pl.ds(pl.multiple_of(which * DH, DH), DH)]


def start_all(pairs, sems):
    copies = [pltpu.make_async_copy(a, b, sems.at[i]) for i, (a, b) in enumerate(pairs)]
    for copy in copies:
        copy.start()
    return copies


def wait_all(copies):
    for copy in copies:
        copy.wait()


def pack_grad_body(core_ref, k_ref, v_ref, lr_ref, own_ref, send_ref, value_ref, rate_ref, sems):
    core = core_ref[0]
    rows = k_ref.shape[0]
    sides = ((send_ref, 1 - core), (own_ref, core))
    pairs = [(half(v_ref, which), value_ref.at[i]) for i, (_, which) in enumerate(sides)]
    pairs += [(half(k_ref, which), ref.at[0]) for ref, which in sides]
    copies = start_all([(lr_ref, rate_ref)] + pairs, sems)
    copies[0].wait()
    for i, (ref, which) in enumerate(sides):
        copies[1 + i].wait()
        rates = jnp.where(which == 0, rate_ref[0:1, :], rate_ref[1:2, :])
        rates = jnp.broadcast_to(rates, (SWA_DH, rows)).T
        for j in range(0, DH, SWA_DH):
            value = value_ref[i, :, j : j + SWA_DH].astype(F32)
            ref[1, :, j : j + SWA_DH] = (-(rates * value)).astype(BF)
    wait_all(copies[3:])


def pack_grad(core, fw_k, fw_v, fw_lr):
    rows = fw_k.shape[0]
    return pl.pallas_call(
        pack_grad_body,
        in_specs=[SM, HBM, HBM, HBM],
        out_specs=[VM, VM],
        out_shape=[on_chip((2, rows, DH)), on_chip((2, rows, DH))],
        scratch_shapes=[
            pltpu.VMEM((2, rows, DH), BF),
            pltpu.VMEM((2, rows), F32),
            pltpu.SemaphoreType.DMA((5,)),
        ],
        compiler_params=PARAMS,
        cost_estimate=cost(rows * 1024, 8 * rows * 1024),
        name="pack_grad",
    )(core, *hbm(fw_k, fw_v, fw_lr.T))


def pick_body(core_ref, gate_ref, up_ref, down_ref, out_ref, sems):
    pairs = [(w.at[core_ref[0]], out_ref.at[i]) for i, w in enumerate((gate_ref, up_ref, down_ref))]
    wait_all(start_all(pairs, sems))


def pick(core, weights):
    return pl.pallas_call(
        pick_body,
        in_specs=[SM] + [HBM] * 3,
        out_specs=VM,
        out_shape=on_chip((3, DH, DH)),
        scratch_shapes=[pltpu.SemaphoreType.DMA((3,))],
        compiler_params=PARAMS,
        cost_estimate=cost(0, 6 * DH * DH),
        name="pick",
    )(core, *hbm(*weights))


def pack_rest_body(core_ref, *refs):
    own_ref, send_ref, sems = refs[4:]
    core = core_ref[0]
    pairs = []
    for ref, which in ((send_ref, 1 - core), (own_ref, core)):
        pairs += [(half(source, which), ref.at[i]) for i, source in enumerate(refs[:4])]
    wait_all(start_all(pairs, sems))


def pack_rest(core, arrays):
    rows = arrays[0].shape[0]
    return pl.pallas_call(
        pack_rest_body,
        in_specs=[SM] + [HBM] * 4,
        out_specs=[VM, VM],
        out_shape=[shape((4, rows, DH)), shape((4, rows, DH))],
        scratch_shapes=[pltpu.SemaphoreType.DMA((8,))],
        compiler_params=PARAMS,
        cost_estimate=cost(0, 16 * rows * 1024),
        name="pack_rest",
    )(core, *hbm(*arrays))


def grads_body(own_ref, got_ref, weight_ref, out_ref):
    keys = jnp.concatenate([own_ref[0], got_ref[0]], axis=0)
    out_grad = jnp.concatenate([own_ref[1], got_ref[1]], axis=0)
    for h in range(DH // HALF):
        cols = slice(h * HALF, (h + 1) * HALF)
        pre_gate = mat(keys, weight_ref[0, :, cols], NN)
        pre_up = mat(keys, weight_ref[1, :, cols], NN)
        hidden_grad = mat(out_grad, weight_ref[2, cols, :], NT)
        sigmoid_gate = jax.nn.sigmoid(pre_gate)
        activated = pre_gate * sigmoid_gate
        hidden = (activated * pre_up).astype(BF)
        slope = sigmoid_gate * (1.0 + pre_gate * (1.0 - sigmoid_gate))
        gate_grad = (hidden_grad * pre_up * slope).astype(BF)
        up_grad = (hidden_grad * activated).astype(BF)
        out_ref[0, :, cols] = mat(keys, gate_grad, TN).astype(BF)
        out_ref[1, :, cols] = mat(keys, up_grad, TN).astype(BF)
        out_ref[2, cols, :] = mat(hidden, out_grad, TN).astype(BF)


def grads(own, got, weights):
    tokens = 2 * own.shape[1]
    return pl.pallas_call(
        grads_body,
        in_specs=[VM] * 3,
        out_specs=VM,
        out_shape=shape((3, DH, DH)),
        compiler_params=PARAMS,
        cost_estimate=cost(12 * tokens * DH * DH, 8 * DH * DH * 2, tokens * DH),
        name="grads",
    )(vmem(own), vmem(got), vmem(weights))


def add_up(in_ref, rows):
    total = in_ref[0, rows].astype(F32)
    for i in range(1, in_ref.shape[0]):
        total += in_ref[i, rows].astype(F32)
    return total.astype(BF)


def sum_body(in_ref, out_ref):
    for r in range(0, out_ref.shape[0], 16):
        rows = slice(r, r + 16)
        out_ref[rows] = add_up(in_ref, rows)


def plane_sum(parts):
    return pl.pallas_call(
        sum_body,
        in_specs=[VM],
        out_specs=VM,
        out_shape=shape(parts.shape[1:]),
        compiler_params=PARAMS,
        cost_estimate=cost(parts.size, 2 * parts.size),
        name="plane_sum",
    )(vmem(parts))


def sum_spread_body(in_ref, out_ref):
    total = add_up(in_ref, slice(None))
    for i in range(out_ref.shape[0]):
        out_ref[i] = total


def sum_spread(parts):
    return pl.pallas_call(
        sum_spread_body,
        in_specs=[VM],
        out_specs=VM,
        out_shape=shape(parts.shape),
        compiler_params=PARAMS,
        cost_estimate=cost(parts.size, 4 * parts.size),
        name="depth_sum",
    )(vmem(parts))


def attend_body(core_ref, chip_ref, own_ref, got_ref, halo_ref, out_ref, *scratch):
    q_ref, k_ref, v_ref, result_ref, sems, out_sem = scratch
    rows = own_ref.shape[1]
    pairs = [(halo_ref.at[0], k_ref.at[:WINDOW]), (halo_ref.at[1], v_ref.at[:WINDOW])]
    for source, which in ((own_ref, core_ref[0]), (got_ref, 1 - core_ref[0])):
        start = pl.multiple_of(which * rows, rows)
        pairs.append((source.at[1], q_ref.at[pl.ds(start, rows)]))
        pairs.append((source.at[2], k_ref.at[pl.ds(start + WINDOW, rows)]))
        pairs.append((source.at[3], v_ref.at[pl.ds(start + WINDOW, rows)]))
    wait_all(start_all(pairs, sems))
    scale = 1.0 / math.sqrt(SWA_DH)
    row = lax.broadcasted_iota(jnp.int32, (WINDOW, 2 * WINDOW), 0)
    col = lax.broadcasted_iota(jnp.int32, (WINDOW, 2 * WINDOW), 1)
    inside = (col > row) & (col <= row + WINDOW)
    first = inside & ((col >= WINDOW) | (chip_ref[0] > 0))
    for b in range(2 * rows // WINDOW):
        seen = first if b == 0 else inside
        queries = slice(b * WINDOW, (b + 1) * WINDOW)
        window = slice(b * WINDOW, (b + 2) * WINDOW)
        for h in range(DH // SWA_DH):
            cols = slice(h * SWA_DH, (h + 1) * SWA_DH)
            scores = mat(q_ref[queries, cols], k_ref[window, cols], NT) * scale
            scores = jnp.where(seen, scores, -jnp.inf)
            exponent = jnp.exp(scores - jnp.max(scores, axis=-1, keepdims=True))
            total = jnp.sum(exponent, axis=-1, keepdims=True)
            probs = (exponent * (1.0 / total)).astype(BF)
            result_ref[queries, cols] = mat(probs, v_ref[window, cols], NN)
    copy = pltpu.make_async_copy(result_ref, out_ref, out_sem)
    copy.start()
    copy.wait()


def attend(core, chip, own, got, halo):
    rows = own.shape[1]
    return pl.pallas_call(
        attend_body,
        in_specs=[SM, SM, HBM, HBM, HBM],
        out_specs=HBM,
        out_shape=pltpu.HBM((2 * rows, DH), F32),
        scratch_shapes=[
            pltpu.VMEM((2 * rows, DH), BF),
            pltpu.VMEM((2 * rows + WINDOW, DH), BF),
            pltpu.VMEM((2 * rows + WINDOW, DH), BF),
            pltpu.VMEM((2 * rows, DH), F32),
            pltpu.SemaphoreType.DMA((8,)),
            pltpu.SemaphoreType.DMA,
        ],
        compiler_params=PARAMS,
        cost_estimate=cost(2 * rows * 8 * WINDOW * DH, 12 * rows * DH, 4 * rows * DH),
        name="window_attention",
    )(core, chip, *hbm(own, got, halo))


def refresh(weight, update):
    initial = weight.astype(F32)
    stepped = initial - update.astype(F32)
    old_norm = jnp.sqrt(jnp.sum(initial * initial, axis=0, keepdims=True) + epsilon)
    new_norm = jnp.sqrt(jnp.sum(stepped * stepped, axis=0, keepdims=True) + epsilon)
    return (stepped * (old_norm / new_norm)).astype(BF)


def finish_body(
    core_ref, yl_ref, sum_ref, gate_ref, up_ref, down_ref, own_ref, got_ref, att_ref, *rest
):
    out_refs = rest[:4]
    all_ref, weight_ref, query_ref, attended_ref, sems = rest[4:]
    core, yl = core_ref[0], yl_ref[0]
    rows = own_ref.shape[1]
    pairs = [(w.at[core], weight_ref.at[i]) for i, w in enumerate((gate_ref, up_ref, down_ref))]
    pairs += [(own_ref.at[0], query_ref.at[0]), (got_ref.at[0], query_ref.at[1])]
    copies = start_all(pairs + [(att_ref, attended_ref)], sems)
    iterates = []
    for m in range(3):
        gradient = sum_ref[m].astype(F32)
        norm_total = jnp.sum(gradient * gradient)
        iterates.append((gradient * (1.0 / jnp.sqrt(norm_total + epsilon))).astype(BF))
    for _ in range(NS_ITERS):
        grams = [mat(x, x, NT).astype(BF) for x in iterates]
        polys = [
            (square_coef * g.astype(F32) + quartic_coef * mat(g, g, NN)).astype(BF) for g in grams
        ]
        iterates = [
            (linear_coef * x.astype(F32) + mat(p, x, NN)).astype(BF)
            for p, x in zip(polys, iterates)
        ]
    wait_all(copies)
    renewed = [refresh(weight_ref[i], x) for i, x in enumerate(iterates)]
    for i, start in enumerate((core * rows, (1 - core) * rows)):
        place = pl.ds(pl.multiple_of(start, rows), rows)
        query_gate = mat(query_ref[i], renewed[0], NN)
        query_up = mat(query_ref[i], renewed[1], NN)
        query_hidden = (query_gate * jax.nn.sigmoid(query_gate) * query_up).astype(BF)
        memory = mat(query_hidden, renewed[2], NN).astype(BF)
        all_ref[place] = (memory.astype(F32) + attended_ref[place]).astype(BF)
    block = out_refs[0].shape[0]
    for i, ref in enumerate(out_refs):
        to_core = 1 - core if i % 2 else core
        to_yl = 1 - yl if i // 2 else yl
        ref[...] = all_ref[pl.ds(pl.multiple_of((to_core * 2 + to_yl) * block, block), block)]


def finish(core, yl, total, gate, up, down, own, got, attended):
    rows = own.shape[1]
    return pl.pallas_call(
        finish_body,
        in_specs=[SM, SM, VM] + [HBM] * 6,
        out_specs=[VM] * 4,
        out_shape=[on_chip((rows // 2, DH))] * 4,
        scratch_shapes=[
            pltpu.VMEM((2 * rows, DH), BF),
            pltpu.VMEM((3, DH, DH), BF),
            pltpu.VMEM((2, rows, DH), BF),
            pltpu.VMEM((2 * rows, DH), F32),
            pltpu.SemaphoreType.DMA((6,)),
        ],
        compiler_params=PARAMS,
        cost_estimate=cost(42 * DH**3, 20 * DH * DH, rows * DH),
        name="finish",
    )(core, yl, vmem(total), *hbm(gate, up, down, own, got, attended))


def unpack_body(core_ref, yl_ref, *refs):
    out_ref = refs[4]
    core, yl = core_ref[0], yl_ref[0]
    for i, ref in enumerate(refs[:4]):
        head = 2 * (1 - yl if i // 2 else yl) + (1 - core if i % 2 else core)
        for which in range(4):

            @pl.when(head == which)
            def _():
                out_ref[:, which * DH : (which + 1) * DH] = ref[...]


def unpack(core, yl, pieces):
    rows = pieces[0].shape[0]
    return pl.pallas_call(
        unpack_body,
        in_specs=[SM, SM] + [VM] * 4,
        out_specs=VM,
        out_shape=shape((rows, 4 * DH)),
        compiler_params=PARAMS,
        cost_estimate=cost(0, 4 * rows * DH * 4),
        name="unpack",
    )(core, yl, *[vmem(p) for p in pieces])


def swap(value, axes):
    return lax.all_to_all(value, axes, split_axis=0, concat_axis=0, tiled=True)


def shards(fw_q, fw_k, fw_v, fw_lr, fast_gate, fast_up, fast_down, attn_q, attn_k, attn_v):
    core = lax.axis_index("core").astype(jnp.int32).reshape(1)
    yl = lax.axis_index("yl").astype(jnp.int32).reshape(1)
    chip = lax.axis_index(CHIPS).astype(jnp.int32).reshape(1)
    pair = [(0, 1), (1, 0)]
    weights = (fast_gate, fast_up, fast_down)
    own, send = pack_grad(core, fw_k, fw_v, fw_lr)
    send, *early = lax.optimization_barrier((send,) + weights)
    partial = grads(own, lax.ppermute(send, "core", pair), pick(core, early))
    plane = lax.axis_size(PLANE)
    depth = lax.axis_size("z")
    partial, *rest = lax.optimization_barrier((partial, fw_q, attn_q, attn_k, attn_v))
    part = swap(partial.reshape(plane, -1, DH), PLANE)
    own, send = pack_rest(core, rest)
    got = lax.ppermute(send, "core", pair)
    part = plane_sum(part)
    part, own, got = lax.optimization_barrier((part, own, got))
    last = jnp.where(core == 1, own[2:, -WINDOW:], got[2:, -WINDOW:])
    chips = lax.axis_size(CHIPS)
    halo = lax.ppermute(last, CHIPS, [(s, s + 1) for s in range(chips - 1)])
    part = swap(part.reshape(depth, -1, DH), "z")
    part = swap(sum_spread(part), "z").reshape(-1, DH)
    part, halo = lax.optimization_barrier((part, halo))
    total = swap(jnp.broadcast_to(part, (plane,) + part.shape), PLANE).reshape(3, DH, DH)
    attended = attend(core, chip, *hbm(own, got, halo))
    kept, to_core, to_chip, to_both = finish(core, yl, total, *weights, own, got, attended)
    pieces = (
        kept,
        lax.ppermute(to_core, "core", pair),
        lax.ppermute(to_chip, "yl", pair),
        lax.ppermute(to_both, QUAD, [(s, 3 - s) for s in range(4)]),
    )
    return unpack(core, yl, pieces)


def solution(mesh):
    fine = Mesh(mesh.devices.reshape(8, 4, 2, 2, 2), ("z", "x", "yh", "core", "yl"))
    ctx = ("z", "x", "yh", "core")
    wide = P(ctx, "yl")
    weight = P("yl", None, None)
    in_specs = (wide, wide, wide, wide, weight, weight, weight, wide, wide, wide)
    out_specs = P(ctx + ("yl",), None)
    return jax.shard_map(shards, mesh=fine, in_specs=in_specs, out_specs=out_specs, check_vma=False)
```

```python
import math

import jax
import jax.numpy as jnp
from jax import lax
from jax.experimental import pallas as pl
from jax.experimental.pallas import tpu as pltpu
from jax.sharding import Mesh, PartitionSpec as P

SWA_DH = 128
WINDOW = 128
NS_ITERS = 2
DH = 512
HALF = 256

linear_coef = 3.4445
square_coef = -4.775
quartic_coef = 2.0315
epsilon = 1e-06


CHIPS = ("z", "plane")
ORDERS = {"plane": [0, 5, 2, 7, 4, 1, 6, 3], "z": [0, 2, 4, 6, 1, 3, 5, 7]}
QUAD = ("core", "yl")

BF = jnp.bfloat16
F32 = jnp.float32
NN, NT, TN = ((1,), (0,)), ((1,), (1,)), ((0,), (0,))


def mat(left, right, dims):
    return lax.dot_general(left, right, (dims, ((), ())), preferred_element_type=F32)


def shape(dims, dtype=BF):
    return jax.ShapeDtypeStruct(dims, dtype)


def cost(flops, nbytes, trans=0):
    return pl.CostEstimate(flops=flops, bytes_accessed=nbytes, transcendentals=trans)


def vmem(value):
    return pltpu.with_memory_space_constraint(value, pltpu.VMEM)


def hbm(*values):
    return [pltpu.with_memory_space_constraint(v, pltpu.HBM) for v in values]


VM = pl.BlockSpec(memory_space=pltpu.VMEM)
SM = pl.BlockSpec(memory_space=pltpu.SMEM)
PARAMS = pltpu.CompilerParams(vmem_limit_bytes=24 * 1024 * 1024)


def on_chip(dims, dtype=BF):
    return pltpu.VMEM(dims, dtype)


HBM = pl.BlockSpec(memory_space=pltpu.HBM)


def half(ref, which):
    return ref.at[:, pl.ds(pl.multiple_of(which * DH, DH), DH)]


def start_all(pairs, sems):
    copies = [pltpu.make_async_copy(a, b, sems.at[i]) for i, (a, b) in enumerate(pairs)]
    for copy in copies:
        copy.start()
    return copies


def wait_all(copies):
    for copy in copies:
        copy.wait()


def pack_grad_body(core_ref, k_ref, v_ref, lr_ref, own_ref, send_ref, value_ref, rate_ref, sems):
    core = core_ref[0]
    rows = k_ref.shape[0]
    sides = ((send_ref, 1 - core), (own_ref, core))
    pairs = [(half(v_ref, which), value_ref.at[i]) for i, (_, which) in enumerate(sides)]
    pairs += [(half(k_ref, which), ref.at[0]) for ref, which in sides]
    copies = start_all([(lr_ref, rate_ref)] + pairs, sems)
    copies[0].wait()
    for i, (ref, which) in enumerate(sides):
        copies[1 + i].wait()
        rates = jnp.where(which == 0, rate_ref[0:1, :], rate_ref[1:2, :])
        rates = jnp.broadcast_to(rates, (SWA_DH, rows)).T
        for j in range(0, DH, SWA_DH):
            value = value_ref[i, :, j : j + SWA_DH].astype(F32)
            ref[1, :, j : j + SWA_DH] = (-(rates * value)).astype(BF)
    wait_all(copies[3:])


def pack_grad(core, fw_k, fw_v, fw_lr):
    rows = fw_k.shape[0]
    return pl.pallas_call(
        pack_grad_body,
        in_specs=[SM, HBM, HBM, HBM],
        out_specs=[VM, VM],
        out_shape=[on_chip((2, rows, DH)), on_chip((2, rows, DH))],
        scratch_shapes=[
            pltpu.VMEM((2, rows, DH), BF),
            pltpu.VMEM((2, rows), F32),
            pltpu.SemaphoreType.DMA((5,)),
        ],
        compiler_params=PARAMS,
        cost_estimate=cost(rows * 1024, 8 * rows * 1024),
        name="pack_grad",
    )(core, *hbm(fw_k, fw_v, fw_lr.T))


def pick_body(core_ref, gate_ref, up_ref, down_ref, out_ref, sems):
    pairs = [(w.at[core_ref[0]], out_ref.at[i]) for i, w in enumerate((gate_ref, up_ref, down_ref))]
    wait_all(start_all(pairs, sems))


def pick(core, weights):
    return pl.pallas_call(
        pick_body,
        in_specs=[SM] + [HBM] * 3,
        out_specs=VM,
        out_shape=on_chip((3, DH, DH)),
        scratch_shapes=[pltpu.SemaphoreType.DMA((3,))],
        compiler_params=PARAMS,
        cost_estimate=cost(0, 6 * DH * DH),
        name="pick",
    )(core, *hbm(*weights))


def pack_rest_body(core_ref, *refs):
    own_ref, send_ref, sems = refs[4:]
    core = core_ref[0]
    pairs = []
    for ref, which in ((send_ref, 1 - core), (own_ref, core)):
        pairs += [(half(source, which), ref.at[i]) for i, source in enumerate(refs[:4])]
    wait_all(start_all(pairs, sems))


def pack_rest(core, arrays):
    rows = arrays[0].shape[0]
    return pl.pallas_call(
        pack_rest_body,
        in_specs=[SM] + [HBM] * 4,
        out_specs=[VM, VM],
        out_shape=[shape((4, rows, DH)), shape((4, rows, DH))],
        scratch_shapes=[pltpu.SemaphoreType.DMA((8,))],
        compiler_params=PARAMS,
        cost_estimate=cost(0, 16 * rows * 1024),
        name="pack_rest",
    )(core, *hbm(*arrays))


def grads_body(own_ref, got_ref, weight_ref, out_ref):
    keys = jnp.concatenate([own_ref[0], got_ref[0]], axis=0)
    out_grad = jnp.concatenate([own_ref[1], got_ref[1]], axis=0)
    for h in range(DH // HALF):
        cols = slice(h * HALF, (h + 1) * HALF)
        pre_gate = mat(keys, weight_ref[0, :, cols], NN)
        pre_up = mat(keys, weight_ref[1, :, cols], NN)
        hidden_grad = mat(out_grad, weight_ref[2, cols, :], NT)
        sigmoid_gate = jax.nn.sigmoid(pre_gate)
        activated = pre_gate * sigmoid_gate
        hidden = (activated * pre_up).astype(BF)
        slope = sigmoid_gate * (1.0 + pre_gate * (1.0 - sigmoid_gate))
        gate_grad = (hidden_grad * pre_up * slope).astype(BF)
        up_grad = (hidden_grad * activated).astype(BF)
        out_ref[0, :, cols] = mat(keys, gate_grad, TN).astype(BF)
        out_ref[1, :, cols] = mat(keys, up_grad, TN).astype(BF)
        out_ref[2, cols, :] = mat(hidden, out_grad, TN).astype(BF)


def grads(own, got, weights):
    tokens = 2 * own.shape[1]
    return pl.pallas_call(
        grads_body,
        in_specs=[VM] * 3,
        out_specs=VM,
        out_shape=shape((3, DH, DH)),
        compiler_params=PARAMS,
        cost_estimate=cost(12 * tokens * DH * DH, 8 * DH * DH * 2, tokens * DH),
        name="grads",
    )(vmem(own), vmem(got), vmem(weights))


def add_up(in_ref, rows):
    total = in_ref[0, rows].astype(F32)
    for i in range(1, in_ref.shape[0]):
        total += in_ref[i, rows].astype(F32)
    return total.astype(BF)


def sum_body(in_ref, out_ref):
    for r in range(0, out_ref.shape[0], 16):
        rows = slice(r, r + 16)
        out_ref[rows] = add_up(in_ref, rows)


def plane_sum(parts):
    return pl.pallas_call(
        sum_body,
        in_specs=[VM],
        out_specs=VM,
        out_shape=shape(parts.shape[1:]),
        compiler_params=PARAMS,
        cost_estimate=cost(parts.size, 2 * parts.size),
        name="plane_sum",
    )(vmem(parts))


def sum_spread_body(in_ref, out_ref):
    total = add_up(in_ref, slice(None))
    for i in range(out_ref.shape[0]):
        out_ref[i] = total


def sum_spread(parts):
    return pl.pallas_call(
        sum_spread_body,
        in_specs=[VM],
        out_specs=VM,
        out_shape=shape(parts.shape),
        compiler_params=PARAMS,
        cost_estimate=cost(parts.size, 4 * parts.size),
        name="depth_sum",
    )(vmem(parts))


def attend_body(core_ref, chip_ref, own_ref, got_ref, halo_ref, out_ref, *scratch):
    q_ref, k_ref, v_ref, result_ref, sems, out_sem = scratch
    rows = own_ref.shape[1]
    pairs = [(halo_ref.at[0], k_ref.at[:WINDOW]), (halo_ref.at[1], v_ref.at[:WINDOW])]
    for source, which in ((own_ref, core_ref[0]), (got_ref, 1 - core_ref[0])):
        start = pl.multiple_of(which * rows, rows)
        pairs.append((source.at[1], q_ref.at[pl.ds(start, rows)]))
        pairs.append((source.at[2], k_ref.at[pl.ds(start + WINDOW, rows)]))
        pairs.append((source.at[3], v_ref.at[pl.ds(start + WINDOW, rows)]))
    wait_all(start_all(pairs, sems))
    scale = 1.0 / math.sqrt(SWA_DH)
    row = lax.broadcasted_iota(jnp.int32, (WINDOW, 2 * WINDOW), 0)
    col = lax.broadcasted_iota(jnp.int32, (WINDOW, 2 * WINDOW), 1)
    inside = (col > row) & (col <= row + WINDOW)
    first = inside & ((col >= WINDOW) | (chip_ref[0] > 0))
    for b in range(2 * rows // WINDOW):
        seen = first if b == 0 else inside
        queries = slice(b * WINDOW, (b + 1) * WINDOW)
        window = slice(b * WINDOW, (b + 2) * WINDOW)
        for h in range(DH // SWA_DH):
            cols = slice(h * SWA_DH, (h + 1) * SWA_DH)
            scores = mat(q_ref[queries, cols], k_ref[window, cols], NT) * scale
            scores = jnp.where(seen, scores, -jnp.inf)
            exponent = jnp.exp(scores - jnp.max(scores, axis=-1, keepdims=True))
            total = jnp.sum(exponent, axis=-1, keepdims=True)
            probs = (exponent * (1.0 / total)).astype(BF)
            result_ref[queries, cols] = mat(probs, v_ref[window, cols], NN)
    copy = pltpu.make_async_copy(result_ref, out_ref, out_sem)
    copy.start()
    copy.wait()


def attend(core, chip, own, got, halo):
    rows = own.shape[1]
    return pl.pallas_call(
        attend_body,
        in_specs=[SM, SM, HBM, HBM, HBM],
        out_specs=HBM,
        out_shape=pltpu.HBM((2 * rows, DH), F32),
        scratch_shapes=[
            pltpu.VMEM((2 * rows, DH), BF),
            pltpu.VMEM((2 * rows + WINDOW, DH), BF),
            pltpu.VMEM((2 * rows + WINDOW, DH), BF),
            pltpu.VMEM((2 * rows, DH), F32),
            pltpu.SemaphoreType.DMA((8,)),
            pltpu.SemaphoreType.DMA,
        ],
        compiler_params=PARAMS,
        cost_estimate=cost(2 * rows * 8 * WINDOW * DH, 12 * rows * DH, 4 * rows * DH),
        name="window_attention",
    )(core, chip, *hbm(own, got, halo))


def refresh(weight, update):
    initial = weight.astype(F32)
    stepped = initial - update.astype(F32)
    old_norm = jnp.sqrt(jnp.sum(initial * initial, axis=0, keepdims=True) + epsilon)
    new_norm = jnp.sqrt(jnp.sum(stepped * stepped, axis=0, keepdims=True) + epsilon)
    return (stepped * (old_norm / new_norm)).astype(BF)


def finish_body(
    core_ref, yl_ref, sum_ref, gate_ref, up_ref, down_ref, own_ref, got_ref, att_ref, *rest
):
    out_refs = rest[:4]
    all_ref, weight_ref, query_ref, attended_ref, sems = rest[4:]
    core, yl = core_ref[0], yl_ref[0]
    rows = own_ref.shape[1]
    pairs = [(w.at[core], weight_ref.at[i]) for i, w in enumerate((gate_ref, up_ref, down_ref))]
    pairs += [(own_ref.at[0], query_ref.at[0]), (got_ref.at[0], query_ref.at[1])]
    copies = start_all(pairs + [(att_ref, attended_ref)], sems)
    iterates = []
    for m in range(3):
        gradient = sum_ref[m].astype(F32)
        norm_total = jnp.sum(gradient * gradient)
        iterates.append((gradient * (1.0 / jnp.sqrt(norm_total + epsilon))).astype(BF))
    for _ in range(NS_ITERS):
        grams = [mat(x, x, NT).astype(BF) for x in iterates]
        polys = [
            (square_coef * g.astype(F32) + quartic_coef * mat(g, g, NN)).astype(BF) for g in grams
        ]
        iterates = [
            (linear_coef * x.astype(F32) + mat(p, x, NN)).astype(BF)
            for p, x in zip(polys, iterates)
        ]
    wait_all(copies)
    renewed = [refresh(weight_ref[i], x) for i, x in enumerate(iterates)]
    for i, start in enumerate((core * rows, (1 - core) * rows)):
        place = pl.ds(pl.multiple_of(start, rows), rows)
        query_gate = mat(query_ref[i], renewed[0], NN)
        query_up = mat(query_ref[i], renewed[1], NN)
        query_hidden = (query_gate * jax.nn.sigmoid(query_gate) * query_up).astype(BF)
        memory = mat(query_hidden, renewed[2], NN).astype(BF)
        all_ref[place] = (memory.astype(F32) + attended_ref[place]).astype(BF)
    block = out_refs[0].shape[0]
    for i, ref in enumerate(out_refs):
        to_core = 1 - core if i % 2 else core
        to_yl = 1 - yl if i // 2 else yl
        ref[...] = all_ref[pl.ds(pl.multiple_of((to_core * 2 + to_yl) * block, block), block)]


def finish(core, yl, total, gate, up, down, own, got, attended):
    rows = own.shape[1]
    return pl.pallas_call(
        finish_body,
        in_specs=[SM, SM, VM] + [HBM] * 6,
        out_specs=[VM] * 4,
        out_shape=[on_chip((rows // 2, DH))] * 4,
        scratch_shapes=[
            pltpu.VMEM((2 * rows, DH), BF),
            pltpu.VMEM((3, DH, DH), BF),
            pltpu.VMEM((2, rows, DH), BF),
            pltpu.VMEM((2 * rows, DH), F32),
            pltpu.SemaphoreType.DMA((6,)),
        ],
        compiler_params=PARAMS,
        cost_estimate=cost(42 * DH**3, 20 * DH * DH, rows * DH),
        name="finish",
    )(core, yl, vmem(total), *hbm(gate, up, down, own, got, attended))


def unpack_body(core_ref, yl_ref, *refs):
    out_ref = refs[4]
    core, yl = core_ref[0], yl_ref[0]
    for i, ref in enumerate(refs[:4]):
        head = 2 * (1 - yl if i // 2 else yl) + (1 - core if i % 2 else core)
        for which in range(4):

            @pl.when(head == which)
            def _():
                out_ref[:, which * DH : (which + 1) * DH] = ref[...]


def unpack(core, yl, pieces):
    rows = pieces[0].shape[0]
    return pl.pallas_call(
        unpack_body,
        in_specs=[SM, SM] + [VM] * 4,
        out_specs=VM,
        out_shape=shape((rows, 4 * DH)),
        compiler_params=PARAMS,
        cost_estimate=cost(0, 4 * rows * DH * 4),
        name="unpack",
    )(core, yl, *[vmem(p) for p in pieces])


def swap(value, axis):
    return lax.all_to_all(
        value, axis, split_axis=0, concat_axis=0, tiled=True, axis_index_groups=[ORDERS[axis]]
    )


def step(fw_q, fw_k, fw_v, fw_lr, fast_gate, fast_up, fast_down, attn_q, attn_k, attn_v):
    core = lax.axis_index("core").astype(jnp.int32).reshape(1)
    yl = lax.axis_index("yl").astype(jnp.int32).reshape(1)
    chip = lax.axis_index(CHIPS).astype(jnp.int32).reshape(1)
    pair = [(0, 1), (1, 0)]
    weights = (fast_gate, fast_up, fast_down)
    own, send = pack_grad(core, fw_k, fw_v, fw_lr)
    send, *early = lax.optimization_barrier((send,) + weights)
    partial = grads(own, lax.ppermute(send, "core", pair), pick(core, early))
    plane = lax.axis_size("plane")
    depth = lax.axis_size("z")
    partial, *rest = lax.optimization_barrier((partial, fw_q, attn_q, attn_k, attn_v))
    part = swap(partial.reshape(plane, -1, DH), "plane")
    own, send = pack_rest(core, rest)
    got = lax.ppermute(send, "core", pair)
    last = jnp.where(core == 1, own[2:, -WINDOW:], got[2:, -WINDOW:])
    part = plane_sum(part)
    part = swap(part.reshape(depth, -1, DH), "z")
    chips = lax.axis_size(CHIPS)
    halo = lax.ppermute(last, CHIPS, [(s, s + 1) for s in range(chips - 1)])
    part = sum_spread(part)
    part = swap(part, "z").reshape(-1, DH)
    spread = jnp.broadcast_to(part, (plane,) + part.shape)
    total = swap(spread, "plane").reshape(3, DH, DH)
    attended = attend(core, chip, *hbm(own, got, halo))
    kept, to_core, to_chip, to_both = finish(core, yl, total, *weights, own, got, attended)
    pieces = (
        kept,
        lax.ppermute(to_core, "core", pair),
        lax.ppermute(to_chip, "yl", pair),
        lax.ppermute(to_both, QUAD, [(s, 3 - s) for s in range(4)]),
    )
    return unpack(core, yl, pieces)


def solution(mesh):
    fine = Mesh(mesh.devices.reshape(8, 8, 2, 2), ("z", "plane", "core", "yl"))
    ctx = ("z", "plane", "core")
    wide = P(ctx, "yl")
    weight = P("yl", None, None)
    in_specs = (wide, wide, wide, wide, weight, weight, weight, wide, wide, wide)
    out_specs = P(ctx + ("yl",), None)
    return jax.shard_map(step, mesh=fine, in_specs=in_specs, out_specs=out_specs, check_vma=False)
```

```python
import math

import jax
import jax.numpy as jnp
from jax import lax
from jax.experimental import pallas as pl
from jax.experimental.pallas import tpu as pltpu
from jax.sharding import Mesh, PartitionSpec as P

SWA_DH = 128
WINDOW = 128
NS_ITERS = 2
DH = 512
HALF = 256

linear_coef = 3.4445
square_coef = -4.775
quartic_coef = 2.0315
epsilon = 1e-06


CHIPS = ("z", "plane")
ORDERS = {"plane": [0, 5, 2, 7, 4, 1, 6, 3], "z": [0, 2, 4, 6, 1, 3, 5, 7]}
QUAD = ("core", "yl")

BF = jnp.bfloat16
F32 = jnp.float32
NN, NT, TN = ((1,), (0,)), ((1,), (1,)), ((0,), (0,))


def mat(left, right, dims):
    return lax.dot_general(left, right, (dims, ((), ())), preferred_element_type=F32)


def shape(dims, dtype=BF):
    return jax.ShapeDtypeStruct(dims, dtype)


def cost(flops, nbytes, trans=0):
    return pl.CostEstimate(flops=flops, bytes_accessed=nbytes, transcendentals=trans)


def vmem(value):
    return pltpu.with_memory_space_constraint(value, pltpu.VMEM)


def hbm(*values):
    return [pltpu.with_memory_space_constraint(v, pltpu.HBM) for v in values]


VM = pl.BlockSpec(memory_space=pltpu.VMEM)
SM = pl.BlockSpec(memory_space=pltpu.SMEM)
PARAMS = pltpu.CompilerParams(vmem_limit_bytes=24 * 1024 * 1024)


def on_chip(dims, dtype=BF):
    return pltpu.VMEM(dims, dtype)


HBM = pl.BlockSpec(memory_space=pltpu.HBM)


def seat(place_ref):
    place = place_ref[0]
    return (place >> 1) & 1, place & 1, place >> 2


def half(ref, which):
    return ref.at[:, pl.ds(pl.multiple_of(which * DH, DH), DH)]


def start_all(pairs, sems):
    copies = [pltpu.make_async_copy(a, b, sems.at[i]) for i, (a, b) in enumerate(pairs)]
    for copy in copies:
        copy.start()
    return copies


def wait_all(copies):
    for copy in copies:
        copy.wait()


def pack_grad_body(place_ref, k_ref, v_ref, lr_ref, own_ref, send_ref, value_ref, rate_ref, sems):
    core, _, _ = seat(place_ref)
    rows = k_ref.shape[0]
    sides = ((send_ref, 1 - core), (own_ref, core))
    pairs = [(half(v_ref, which), value_ref.at[i]) for i, (_, which) in enumerate(sides)]
    pairs += [(half(k_ref, which), ref.at[0]) for ref, which in sides]
    copies = start_all([(lr_ref, rate_ref)] + pairs, sems)
    copies[0].wait()
    for i, (ref, which) in enumerate(sides):
        copies[1 + i].wait()
        rates = jnp.where(which == 0, rate_ref[0:1, :], rate_ref[1:2, :])
        rates = jnp.broadcast_to(rates, (SWA_DH, rows)).T
        for j in range(0, DH, SWA_DH):
            value = value_ref[i, :, j : j + SWA_DH].astype(F32)
            ref[1, :, j : j + SWA_DH] = (-(rates * value)).astype(BF)
    wait_all(copies[3:])


def pack_grad(place, fw_k, fw_v, fw_lr):
    rows = fw_k.shape[0]
    return pl.pallas_call(
        pack_grad_body,
        in_specs=[SM, HBM, HBM, HBM],
        out_specs=[VM, VM],
        out_shape=[on_chip((2, rows, DH)), on_chip((2, rows, DH))],
        scratch_shapes=[
            pltpu.VMEM((2, rows, DH), BF),
            pltpu.VMEM((2, rows), F32),
            pltpu.SemaphoreType.DMA((5,)),
        ],
        compiler_params=PARAMS,
        cost_estimate=cost(rows * 1024, 8 * rows * 1024),
        name="pack_grad",
    )(place, *hbm(fw_k, fw_v, fw_lr.T))


def pick_body(place_ref, *refs):
    out_ref, send_ref, sems = refs[7:]
    core, _, _ = seat(place_ref)
    pairs = [(half(source, 1 - core), send_ref.at[i]) for i, source in enumerate(refs[3:7])]
    pairs += [(w.at[core], out_ref.at[i]) for i, w in enumerate(refs[:3])]
    wait_all(start_all(pairs, sems))


def pick(place, weights, arrays):
    rows = arrays[0].shape[0]
    return pl.pallas_call(
        pick_body,
        in_specs=[SM] + [HBM] * 7,
        out_specs=[VM, VM],
        out_shape=[on_chip((3, DH, DH)), on_chip((4, rows, DH))],
        scratch_shapes=[pltpu.SemaphoreType.DMA((7,))],
        compiler_params=PARAMS,
        cost_estimate=cost(0, 6 * DH * DH + 8 * rows * DH),
        name="pick",
    )(place, *hbm(*weights, *arrays))


def grads_body(own_ref, got_ref, weight_ref, out_ref):
    keys = jnp.concatenate([own_ref[0], got_ref[0]], axis=0)
    out_grad = jnp.concatenate([own_ref[1], got_ref[1]], axis=0)
    for h in range(DH // HALF):
        cols = slice(h * HALF, (h + 1) * HALF)
        pre_gate = mat(keys, weight_ref[0, :, cols], NN)
        pre_up = mat(keys, weight_ref[1, :, cols], NN)
        hidden_grad = mat(out_grad, weight_ref[2, cols, :], NT)
        sigmoid_gate = jax.nn.sigmoid(pre_gate)
        activated = pre_gate * sigmoid_gate
        hidden = (activated * pre_up).astype(BF)
        slope = sigmoid_gate * (1.0 + pre_gate * (1.0 - sigmoid_gate))
        gate_grad = (hidden_grad * pre_up * slope).astype(BF)
        up_grad = (hidden_grad * activated).astype(BF)
        out_ref[0, :, cols] = mat(keys, gate_grad, TN).astype(BF)
        out_ref[1, :, cols] = mat(keys, up_grad, TN).astype(BF)
        out_ref[2, cols, :] = mat(hidden, out_grad, TN).astype(BF)


def grads(own, got, weights):
    tokens = 2 * own.shape[1]
    return pl.pallas_call(
        grads_body,
        in_specs=[VM] * 3,
        out_specs=VM,
        out_shape=on_chip((3, DH, DH)),
        compiler_params=PARAMS,
        cost_estimate=cost(12 * tokens * DH * DH, 8 * DH * DH * 2, tokens * DH),
        name="grads",
    )(vmem(own), vmem(got), vmem(weights))


def add_up(in_ref, rows):
    total = in_ref[0, rows].astype(F32)
    for i in range(1, in_ref.shape[0]):
        total += in_ref[i, rows].astype(F32)
    return total.astype(BF)


def sum_body(in_ref, out_ref):
    for r in range(0, out_ref.shape[0], 16):
        rows = slice(r, r + 16)
        out_ref[rows] = add_up(in_ref, rows)


def plane_sum(parts):
    return pl.pallas_call(
        sum_body,
        in_specs=[VM],
        out_specs=VM,
        out_shape=shape(parts.shape[1:]),
        compiler_params=PARAMS,
        cost_estimate=cost(parts.size, 2 * parts.size),
        name="plane_sum",
    )(vmem(parts))


def tail_body(place_ref, k_ref, v_ref, got_ref, out_ref, sems):
    core, _, _ = seat(place_ref)
    tail = pl.ds(k_ref.shape[0] - WINDOW, WINDOW)
    kept = [(half(ref, 1).at[tail], out_ref.at[i]) for i, ref in enumerate((k_ref, v_ref))]
    other = [(got_ref.at[2 + i, tail], out_ref.at[i]) for i in range(2)]
    pl.when(core == 1)(lambda: wait_all(start_all(kept, sems)))
    pl.when(core != 1)(lambda: wait_all(start_all(other, sems)))


def last_rows(place, attn_k, attn_v, got):
    return pl.pallas_call(
        tail_body,
        in_specs=[SM, HBM, HBM, HBM],
        out_specs=VM,
        out_shape=on_chip((2, WINDOW, DH)),
        scratch_shapes=[pltpu.SemaphoreType.DMA((2,))],
        compiler_params=PARAMS,
        cost_estimate=cost(0, 8 * WINDOW * DH),
        name="tail",
    )(place, *hbm(attn_k, attn_v, got))


def sum_spread_body(in_ref, out_ref):
    total = add_up(in_ref, slice(None))
    for i in range(out_ref.shape[0]):
        out_ref[i] = total


def sum_spread(parts):
    return pl.pallas_call(
        sum_spread_body,
        in_specs=[VM],
        out_specs=VM,
        out_shape=shape(parts.shape),
        compiler_params=PARAMS,
        cost_estimate=cost(parts.size, 4 * parts.size),
        name="depth_sum",
    )(vmem(parts))


def attend_body(place_ref, own_q, own_k, own_v, got_ref, halo_ref, out_ref, *scratch):
    q_ref, k_ref, v_ref, result_ref, sems, out_sem = scratch
    core, _, chip = seat(place_ref)
    rows = own_q.shape[0]
    pairs = [(halo_ref.at[0], k_ref.at[:WINDOW]), (halo_ref.at[1], v_ref.at[:WINDOW])]
    own = [half(ref, core) for ref in (own_q, own_k, own_v)]
    for sources, which in ((own, core), ([got_ref.at[i] for i in (1, 2, 3)], 1 - core)):
        start = pl.multiple_of(which * rows, rows)
        pairs.append((sources[0], q_ref.at[pl.ds(start, rows)]))
        pairs.append((sources[1], k_ref.at[pl.ds(start + WINDOW, rows)]))
        pairs.append((sources[2], v_ref.at[pl.ds(start + WINDOW, rows)]))
    wait_all(start_all(pairs, sems))
    scale = 1.0 / math.sqrt(SWA_DH)
    row = lax.broadcasted_iota(jnp.int32, (WINDOW, 2 * WINDOW), 0)
    col = lax.broadcasted_iota(jnp.int32, (WINDOW, 2 * WINDOW), 1)
    inside = (col > row) & (col <= row + WINDOW)
    first = inside & ((col >= WINDOW) | (chip > 0))
    for b in range(2 * rows // WINDOW):
        seen = first if b == 0 else inside
        queries = slice(b * WINDOW, (b + 1) * WINDOW)
        window = slice(b * WINDOW, (b + 2) * WINDOW)
        for h in range(DH // SWA_DH):
            cols = slice(h * SWA_DH, (h + 1) * SWA_DH)
            scores = mat(q_ref[queries, cols], k_ref[window, cols], NT) * scale
            scores = jnp.where(seen, scores, -jnp.inf)
            exponent = jnp.exp(scores - jnp.max(scores, axis=-1, keepdims=True))
            total = jnp.sum(exponent, axis=-1, keepdims=True)
            probs = (exponent * (1.0 / total)).astype(BF)
            result_ref[queries, cols] = mat(probs, v_ref[window, cols], NN)
    copy = pltpu.make_async_copy(result_ref, out_ref, out_sem)
    copy.start()
    copy.wait()


def attend(place, own, got, halo):
    rows = got.shape[1]
    return pl.pallas_call(
        attend_body,
        in_specs=[SM, HBM, HBM, HBM, HBM, VM],
        out_specs=HBM,
        out_shape=pltpu.HBM((2 * rows, DH), F32),
        scratch_shapes=[
            pltpu.VMEM((2 * rows, DH), BF),
            pltpu.VMEM((2 * rows + WINDOW, DH), BF),
            pltpu.VMEM((2 * rows + WINDOW, DH), BF),
            pltpu.VMEM((2 * rows, DH), F32),
            pltpu.SemaphoreType.DMA((8,)),
            pltpu.SemaphoreType.DMA,
        ],
        compiler_params=PARAMS,
        cost_estimate=cost(2 * rows * 8 * WINDOW * DH, 12 * rows * DH, 4 * rows * DH),
        name="window_attention",
    )(place, *hbm(*own, got), vmem(halo))


def refresh(weight, update):
    initial = weight.astype(F32)
    stepped = initial - update.astype(F32)
    old_norm = jnp.sqrt(jnp.sum(initial * initial, axis=0, keepdims=True) + epsilon)
    new_norm = jnp.sqrt(jnp.sum(stepped * stepped, axis=0, keepdims=True) + epsilon)
    return (stepped * (old_norm / new_norm)).astype(BF)


def finish_body(
    place_ref, sum_ref, gate_ref, up_ref, down_ref, own_ref, got_ref, att_ref, *rest
):
    out_refs = rest[:4]
    all_ref, weight_ref, query_ref, attended_ref, sems = rest[4:]
    core, yl, _ = seat(place_ref)
    rows = own_ref.shape[0]
    pairs = [(w.at[core], weight_ref.at[i]) for i, w in enumerate((gate_ref, up_ref, down_ref))]
    pairs += [(half(own_ref, core), query_ref.at[0]), (got_ref.at[0], query_ref.at[1])]
    copies = start_all(pairs + [(att_ref, attended_ref)], sems)
    iterates = []
    for m in range(3):
        gradient = sum_ref[m].astype(F32)
        norm_total = jnp.sum(gradient * gradient)
        iterates.append((gradient * (1.0 / jnp.sqrt(norm_total + epsilon))).astype(BF))
    for _ in range(NS_ITERS):
        grams = [mat(x, x, NT).astype(BF) for x in iterates]
        polys = [
            (square_coef * g.astype(F32) + quartic_coef * mat(g, g, NN)).astype(BF) for g in grams
        ]
        iterates = [
            (linear_coef * x.astype(F32) + mat(p, x, NN)).astype(BF)
            for p, x in zip(polys, iterates)
        ]
    wait_all(copies)
    renewed = [refresh(weight_ref[i], x) for i, x in enumerate(iterates)]
    for i, start in enumerate((core * rows, (1 - core) * rows)):
        place = pl.ds(pl.multiple_of(start, rows), rows)
        query_gate = mat(query_ref[i], renewed[0], NN)
        query_up = mat(query_ref[i], renewed[1], NN)
        query_hidden = (query_gate * jax.nn.sigmoid(query_gate) * query_up).astype(BF)
        memory = mat(query_hidden, renewed[2], NN).astype(BF)
        all_ref[place] = (memory.astype(F32) + attended_ref[place]).astype(BF)
    block = out_refs[0].shape[0]
    for i, ref in enumerate(out_refs):
        to_core = 1 - core if i % 2 else core
        to_yl = 1 - yl if i // 2 else yl
        ref[...] = all_ref[pl.ds(pl.multiple_of((to_core * 2 + to_yl) * block, block), block)]


def finish(place, total, gate, up, down, own, got, attended):
    rows = own.shape[0]
    return pl.pallas_call(
        finish_body,
        in_specs=[SM, VM] + [HBM] * 6,
        out_specs=[VM] * 4,
        out_shape=[on_chip((rows // 2, DH))] * 4,
        scratch_shapes=[
            pltpu.VMEM((2 * rows, DH), BF),
            pltpu.VMEM((3, DH, DH), BF),
            pltpu.VMEM((2, rows, DH), BF),
            pltpu.VMEM((2 * rows, DH), F32),
            pltpu.SemaphoreType.DMA((6,)),
        ],
        compiler_params=PARAMS,
        cost_estimate=cost(42 * DH**3, 20 * DH * DH, rows * DH),
        name="finish",
    )(place, vmem(total), *hbm(gate, up, down, own, got, attended))


def unpack_body(place_ref, *refs):
    out_ref = refs[4]
    core, yl, _ = seat(place_ref)
    for i, ref in enumerate(refs[:4]):
        head = 2 * (1 - yl if i // 2 else yl) + (1 - core if i % 2 else core)
        for which in range(4):

            @pl.when(head == which)
            def _():
                out_ref[:, which * DH : (which + 1) * DH] = ref[...]


def unpack(place, pieces):
    rows = pieces[0].shape[0]
    return pl.pallas_call(
        unpack_body,
        in_specs=[SM] + [VM] * 4,
        out_specs=VM,
        out_shape=shape((rows, 4 * DH)),
        compiler_params=PARAMS,
        cost_estimate=cost(0, 4 * rows * DH * 4),
        name="unpack",
    )(place, *[vmem(p) for p in pieces])


def swap(value, axis):
    return lax.all_to_all(
        value, axis, split_axis=0, concat_axis=0, tiled=True, axis_index_groups=[ORDERS[axis]]
    )


def step(fw_q, fw_k, fw_v, fw_lr, fast_gate, fast_up, fast_down, attn_q, attn_k, attn_v):
    place = lax.axis_index(CHIPS + QUAD).astype(jnp.int32).reshape(1)
    pair = [(0, 1), (1, 0)]
    weights = (fast_gate, fast_up, fast_down)
    rest = (fw_q, attn_q, attn_k, attn_v)
    own, send = pack_grad(place, fw_k, fw_v, fw_lr)
    send, *early = lax.optimization_barrier((send,) + weights)
    moved = lax.ppermute(send, "core", pair)
    picked, send = pick(place, early, rest)
    got = lax.ppermute(send, "core", pair)
    partial = grads(own, moved, picked)
    plane = lax.axis_size("plane")
    depth = lax.axis_size("z")
    part = swap(partial.reshape(plane, -1, DH), "plane")
    part = plane_sum(part)
    part = swap(part.reshape(depth, -1, DH), "z")
    last = last_rows(place, attn_k, attn_v, got)
    chips = lax.axis_size(CHIPS)
    halo = lax.ppermute(last, CHIPS, [(s, s + 1) for s in range(chips - 1)])
    part = sum_spread(part)
    part = swap(part, "z").reshape(-1, DH)
    spread = jnp.broadcast_to(part, (plane,) + part.shape)
    total = swap(spread, "plane").reshape(3, DH, DH)
    attended = attend(place, rest[1:], got, halo)
    kept, to_core, to_chip, to_both = finish(place, total, *weights, fw_q, got, attended)
    from_chip = lax.ppermute(to_chip, "yl", pair)
    from_both = lax.ppermute(to_both, QUAD, [(s, 3 - s) for s in range(4)])
    from_core = lax.ppermute(to_core, "core", pair)
    pieces = (kept, from_core, from_chip, from_both)
    return unpack(place, pieces)


def solution(mesh):
    fine = Mesh(mesh.devices.reshape(8, 8, 2, 2), ("z", "plane", "core", "yl"))
    ctx = ("z", "plane", "core")
    wide = P(ctx, "yl")
    weight = P("yl", None, None)
    in_specs = (wide, wide, wide, wide, weight, weight, weight, wide, wide, wide)
    out_specs = P(ctx + ("yl",), None)
    return jax.shard_map(step, mesh=fine, in_specs=in_specs, out_specs=out_specs, check_vma=False)
```

```python
import math

import jax
import jax.numpy as jnp
from jax import lax
from jax.experimental import pallas as pl
from jax.experimental.pallas import tpu as pltpu
from jax.sharding import Mesh, PartitionSpec as P

SWA_DH = 128
WINDOW = 128
NS_ITERS = 2
DH = 512
HALF = 256
PARTS = 8

linear_coef = 3.4445
square_coef = -4.775
quartic_coef = 2.0315
epsilon = 1e-06


CHIPS = ("z", "plane")
ORDERS = {"plane": [0, 5, 2, 7, 4, 1, 6, 3], "z": [7, 6, 5, 4, 3, 2, 1, 0]}
QUAD = ("core", "yl")

BF = jnp.bfloat16
F32 = jnp.float32
NN, NT, TN = ((1,), (0,)), ((1,), (1,)), ((0,), (0,))


def mat(left, right, dims):
    return lax.dot_general(left, right, (dims, ((), ())), preferred_element_type=F32)


def shape(dims, dtype=BF):
    return jax.ShapeDtypeStruct(dims, dtype)


def cost(flops, nbytes, trans=0):
    return pl.CostEstimate(flops=flops, bytes_accessed=nbytes, transcendentals=trans)


def vmem(value):
    return pltpu.with_memory_space_constraint(value, pltpu.VMEM)


def hbm(*values):
    return [pltpu.with_memory_space_constraint(v, pltpu.HBM) for v in values]


VM = pl.BlockSpec(memory_space=pltpu.VMEM)
SM = pl.BlockSpec(memory_space=pltpu.SMEM)
PARAMS = pltpu.CompilerParams(vmem_limit_bytes=24 * 1024 * 1024)


def on_chip(dims, dtype=BF):
    return pltpu.VMEM(dims, dtype)


HBM = pl.BlockSpec(memory_space=pltpu.HBM)


def seat(place_ref):
    place = place_ref[0]
    return (place >> 1) & 1, place & 1, place >> 2


def half(ref, which):
    return ref.at[:, pl.ds(pl.multiple_of(which * DH, DH), DH)]


def start_all(pairs, sems):
    copies = [pltpu.make_async_copy(a, b, sems.at[i]) for i, (a, b) in enumerate(pairs)]
    for copy in copies:
        copy.start()
    return copies


def wait_all(copies):
    for copy in copies:
        copy.wait()


def pack_grad_body(place_ref, k_ref, v_ref, lr_ref, own_ref, send_ref, value_ref, rate_ref, sems):
    core, _, _ = seat(place_ref)
    rows = k_ref.shape[0]
    sides = ((send_ref, 1 - core), (own_ref, core))
    pairs = [(half(v_ref, which), value_ref.at[i]) for i, (_, which) in enumerate(sides)]
    pairs += [(half(k_ref, which), ref.at[0]) for ref, which in sides]
    copies = start_all([(lr_ref, rate_ref)] + pairs, sems)
    copies[0].wait()
    for i, (ref, which) in enumerate(sides):
        copies[1 + i].wait()
        rates = jnp.where(which == 0, rate_ref[0:1, :], rate_ref[1:2, :])
        rates = jnp.broadcast_to(rates, (SWA_DH, rows)).T
        for j in range(0, DH, SWA_DH):
            value = value_ref[i, :, j : j + SWA_DH].astype(F32)
            ref[1, :, j : j + SWA_DH] = (-(rates * value)).astype(BF)
    wait_all(copies[3:])


def pack_grad(place, fw_k, fw_v, fw_lr):
    rows = fw_k.shape[0]
    return pl.pallas_call(
        pack_grad_body,
        in_specs=[SM, HBM, HBM, HBM],
        out_specs=[VM, VM],
        out_shape=[on_chip((2, rows, DH)), on_chip((2, rows, DH))],
        scratch_shapes=[
            pltpu.VMEM((2, rows, DH), BF),
            pltpu.VMEM((2, rows), F32),
            pltpu.SemaphoreType.DMA((5,)),
        ],
        compiler_params=PARAMS,
        cost_estimate=cost(rows * 1024, 8 * rows * 1024),
        name="pack_grad",
    )(place, *hbm(fw_k, fw_v, fw_lr.T))


def pick_body(place_ref, *refs):
    out_ref, send_ref, sems = refs[7:]
    core, _, _ = seat(place_ref)
    pairs = [(half(source, 1 - core), send_ref.at[i]) for i, source in enumerate(refs[3:7])]
    pairs += [(w.at[core], out_ref.at[i]) for i, w in enumerate(refs[:3])]
    wait_all(start_all(pairs, sems))


def pick(place, weights, arrays):
    rows = arrays[0].shape[0]
    return pl.pallas_call(
        pick_body,
        in_specs=[SM] + [HBM] * 7,
        out_specs=[VM, VM],
        out_shape=[on_chip((3, DH, DH)), on_chip((4, rows, DH))],
        scratch_shapes=[pltpu.SemaphoreType.DMA((7,))],
        compiler_params=PARAMS,
        cost_estimate=cost(0, 6 * DH * DH + 8 * rows * DH),
        name="pick",
    )(place, *hbm(*weights, *arrays))


def grads_body(own_ref, got_ref, weight_ref, out_ref):
    keys = jnp.concatenate([own_ref[0], got_ref[0]], axis=0)
    out_grad = jnp.concatenate([own_ref[1], got_ref[1]], axis=0)
    for h in range(DH // HALF):
        cols = slice(h * HALF, (h + 1) * HALF)
        pre_gate = mat(keys, weight_ref[0, :, cols], NN)
        pre_up = mat(keys, weight_ref[1, :, cols], NN)
        hidden_grad = mat(out_grad, weight_ref[2, cols, :], NT)
        sigmoid_gate = jax.nn.sigmoid(pre_gate)
        activated = pre_gate * sigmoid_gate
        hidden = (activated * pre_up).astype(BF)
        slope = sigmoid_gate * (1.0 + pre_gate * (1.0 - sigmoid_gate))
        gate_grad = (hidden_grad * pre_up * slope).astype(BF)
        up_grad = (hidden_grad * activated).astype(BF)
        out_ref[:, 0, :, cols] = mat(keys, gate_grad, TN).astype(BF).reshape(PARTS, -1, HALF)
        out_ref[:, 1, :, cols] = mat(keys, up_grad, TN).astype(BF).reshape(PARTS, -1, HALF)
        down = mat(hidden, out_grad, TN).astype(BF).reshape(PARTS // 2, -1, DH)
        out_ref[h * PARTS // 2 : (h + 1) * PARTS // 2, 2] = down


def grads(own, got, weights):
    tokens = 2 * own.shape[1]
    return pl.pallas_call(
        grads_body,
        in_specs=[VM] * 3,
        out_specs=VM,
        out_shape=on_chip((PARTS, 3, DH // PARTS, DH)),
        compiler_params=PARAMS,
        cost_estimate=cost(12 * tokens * DH * DH, 8 * DH * DH * 2, tokens * DH),
        name="grads",
    )(vmem(own), vmem(got), vmem(weights))


def add_up(in_ref, rows):
    total = in_ref[0, rows].astype(F32)
    for i in range(1, in_ref.shape[0]):
        total += in_ref[i, rows].astype(F32)
    return total.astype(BF)


def sum_body(in_ref, out_ref):
    for r in range(0, out_ref.shape[0], 16):
        rows = slice(r, r + 16)
        out_ref[rows] = add_up(in_ref, rows)


def plane_sum(parts):
    return pl.pallas_call(
        sum_body,
        in_specs=[VM],
        out_specs=VM,
        out_shape=shape(parts.shape[1:]),
        compiler_params=PARAMS,
        cost_estimate=cost(parts.size, 2 * parts.size),
        name="plane_sum",
    )(vmem(parts))


def tail_body(place_ref, k_ref, v_ref, got_ref, out_ref, sems):
    core, _, _ = seat(place_ref)
    tail = pl.ds(k_ref.shape[0] - WINDOW, WINDOW)
    kept = [(half(ref, 1).at[tail], out_ref.at[i]) for i, ref in enumerate((k_ref, v_ref))]
    other = [(got_ref.at[2 + i, tail], out_ref.at[i]) for i in range(2)]
    pl.when(core == 1)(lambda: wait_all(start_all(kept, sems)))
    pl.when(core != 1)(lambda: wait_all(start_all(other, sems)))


def last_rows(place, attn_k, attn_v, got):
    return pl.pallas_call(
        tail_body,
        in_specs=[SM, HBM, HBM, HBM],
        out_specs=VM,
        out_shape=on_chip((2, WINDOW, DH)),
        scratch_shapes=[pltpu.SemaphoreType.DMA((2,))],
        compiler_params=PARAMS,
        cost_estimate=cost(0, 8 * WINDOW * DH),
        name="tail",
    )(place, *hbm(attn_k, attn_v, got))


def sum_spread_body(in_ref, out_ref):
    total = add_up(in_ref, slice(None))
    for i in range(out_ref.shape[0]):
        out_ref[i] = total


def sum_spread(parts):
    return pl.pallas_call(
        sum_spread_body,
        in_specs=[VM],
        out_specs=VM,
        out_shape=shape(parts.shape),
        compiler_params=PARAMS,
        cost_estimate=cost(parts.size, 4 * parts.size),
        name="depth_sum",
    )(vmem(parts))


def attend_body(place_ref, own_q, own_k, own_v, got_ref, halo_ref, out_ref, *scratch):
    q_ref, k_ref, v_ref, result_ref, sems, out_sem = scratch
    core, _, chip = seat(place_ref)
    rows = own_q.shape[0]
    pairs = [(halo_ref.at[0], k_ref.at[:WINDOW]), (halo_ref.at[1], v_ref.at[:WINDOW])]
    own = [half(ref, core) for ref in (own_q, own_k, own_v)]
    for sources, which in ((own, core), ([got_ref.at[i] for i in (1, 2, 3)], 1 - core)):
        start = pl.multiple_of(which * rows, rows)
        pairs.append((sources[0], q_ref.at[pl.ds(start, rows)]))
        pairs.append((sources[1], k_ref.at[pl.ds(start + WINDOW, rows)]))
        pairs.append((sources[2], v_ref.at[pl.ds(start + WINDOW, rows)]))
    wait_all(start_all(pairs, sems))
    scale = 1.0 / math.sqrt(SWA_DH)
    row = lax.broadcasted_iota(jnp.int32, (WINDOW, 2 * WINDOW), 0)
    col = lax.broadcasted_iota(jnp.int32, (WINDOW, 2 * WINDOW), 1)
    inside = (col > row) & (col <= row + WINDOW)
    first = inside & ((col >= WINDOW) | (chip > 0))
    for b in range(2 * rows // WINDOW):
        seen = first if b == 0 else inside
        queries = slice(b * WINDOW, (b + 1) * WINDOW)
        window = slice(b * WINDOW, (b + 2) * WINDOW)
        for h in range(DH // SWA_DH):
            cols = slice(h * SWA_DH, (h + 1) * SWA_DH)
            scores = mat(q_ref[queries, cols], k_ref[window, cols], NT) * scale
            scores = jnp.where(seen, scores, -jnp.inf)
            exponent = jnp.exp(scores - jnp.max(scores, axis=-1, keepdims=True))
            total = jnp.sum(exponent, axis=-1, keepdims=True)
            probs = (exponent * (1.0 / total)).astype(BF)
            result_ref[queries, cols] = mat(probs, v_ref[window, cols], NN)
    copy = pltpu.make_async_copy(result_ref, out_ref, out_sem)
    copy.start()
    copy.wait()


def attend(place, own, got, halo):
    rows = got.shape[1]
    return pl.pallas_call(
        attend_body,
        in_specs=[SM, HBM, HBM, HBM, HBM, VM],
        out_specs=HBM,
        out_shape=pltpu.HBM((2 * rows, DH), F32),
        scratch_shapes=[
            pltpu.VMEM((2 * rows, DH), BF),
            pltpu.VMEM((2 * rows + WINDOW, DH), BF),
            pltpu.VMEM((2 * rows + WINDOW, DH), BF),
            pltpu.VMEM((2 * rows, DH), F32),
            pltpu.SemaphoreType.DMA((8,)),
            pltpu.SemaphoreType.DMA,
        ],
        compiler_params=PARAMS,
        cost_estimate=cost(2 * rows * 8 * WINDOW * DH, 12 * rows * DH, 4 * rows * DH),
        name="window_attention",
    )(place, *hbm(*own, got), vmem(halo))


def refresh(weight, update):
    initial = weight.astype(F32)
    stepped = initial - update.astype(F32)
    old_norm = jnp.sqrt(jnp.sum(initial * initial, axis=0, keepdims=True) + epsilon)
    new_norm = jnp.sqrt(jnp.sum(stepped * stepped, axis=0, keepdims=True) + epsilon)
    return (stepped * (old_norm / new_norm)).astype(BF)


MOVES = [(across, flip) for across in range(4) for flip in range(2)]


def move_along(across, flip):
    def target(p):
        return ((p // 2 + across) % 4) * 2 + (p % 2 ^ flip)

    return [(p, target(p)) for p in range(PARTS)]


def orthogonal(gradients):
    iterates = []
    for gradient in gradients:
        gradient = gradient.reshape(DH, DH).astype(F32)
        norm_total = jnp.sum(gradient * gradient)
        iterates.append((gradient * (1.0 / jnp.sqrt(norm_total + epsilon))).astype(BF))
    for _ in range(NS_ITERS):
        grams = [mat(x, x, NT).astype(BF) for x in iterates]
        polys = [
            (square_coef * g.astype(F32) + quartic_coef * mat(g, g, NN)).astype(BF) for g in grams
        ]
        iterates = [
            (linear_coef * x.astype(F32) + mat(p, x, NN)).astype(BF)
            for p, x in zip(polys, iterates)
        ]
    return iterates


def open_body(place_ref, sum_ref, gate_ref, up_ref, own_ref, got_ref, out_ref, *scratch):
    weight_ref, query_ref, sems = scratch
    core, _, _ = seat(place_ref)
    rows = own_ref.shape[0]
    pairs = [(w.at[core], weight_ref.at[i]) for i, w in enumerate((gate_ref, up_ref))]
    for source, which in ((half(own_ref, core), core), (got_ref.at[0], 1 - core)):
        place = pl.ds(pl.multiple_of(which * rows, rows), rows)
        pairs.append((source, query_ref.at[place]))
    copies = start_all(pairs, sems)
    iterates = orthogonal([sum_ref[:, 0], sum_ref[:, 1]])
    wait_all(copies)
    gate, up = (refresh(weight_ref[i], x) for i, x in enumerate(iterates))
    query_gate = mat(query_ref[...], gate, NN)
    query_up = mat(query_ref[...], up, NN)
    out_ref[...] = (query_gate * jax.nn.sigmoid(query_gate) * query_up).astype(BF)


def open_answer(place, total, gate, up, own, got):
    rows = own.shape[0]
    return pl.pallas_call(
        open_body,
        in_specs=[SM, VM] + [HBM] * 4,
        out_specs=VM,
        out_shape=on_chip((2 * rows, DH)),
        scratch_shapes=[
            pltpu.VMEM((2, DH, DH), BF),
            pltpu.VMEM((2 * rows, DH), BF),
            pltpu.SemaphoreType.DMA((4,)),
        ],
        compiler_params=PARAMS,
        cost_estimate=cost(28 * DH**3, 12 * DH * DH, rows * DH),
        name="open_answer",
    )(place, vmem(total), *hbm(gate, up, own, got))


def close_body(place_ref, down_ref, hidden_ref, att_ref, *rest):
    part_refs, out_refs = rest[:PARTS], rest[PARTS : PARTS + 4]
    all_ref, sum_ref, weight_ref, attended_ref, sems = rest[PARTS + 4 :]
    core, yl, chip = seat(place_ref)
    copies = start_all([(down_ref.at[core], weight_ref), (att_ref, attended_ref)], sems)
    x, yh = (chip >> 1) & 3, chip & 1
    for ref, (across, flip) in zip(part_refs, MOVES):
        source = ((x - across) & 3) * 2 + (yh ^ flip)
        sum_ref[source ^ ((source & 1) * 4)] = ref[...]
    (iterate,) = orthogonal([sum_ref[...]])
    wait_all(copies)
    down = refresh(weight_ref[...], iterate)
    memory = mat(hidden_ref[...], down, NN).astype(BF)
    all_ref[...] = (memory.astype(F32) + attended_ref[...]).astype(BF)
    block = out_refs[0].shape[0]
    for i, ref in enumerate(out_refs):
        to_core = 1 - core if i % 2 else core
        to_yl = 1 - yl if i // 2 else yl
        ref[...] = all_ref[pl.ds(pl.multiple_of((to_core * 2 + to_yl) * block, block), block)]


def close_answer(place, parts, down, hidden, attended):
    rows = hidden.shape[0]
    return pl.pallas_call(
        close_body,
        in_specs=[SM, HBM, VM, HBM] + [VM] * PARTS,
        out_specs=[VM] * 4,
        out_shape=[on_chip((rows // 4, DH))] * 4,
        scratch_shapes=[
            pltpu.VMEM((rows, DH), BF),
            pltpu.VMEM((PARTS, DH // PARTS, DH), BF),
            pltpu.VMEM((DH, DH), BF),
            pltpu.VMEM((rows, DH), F32),
            pltpu.SemaphoreType.DMA((2,)),
        ],
        compiler_params=PARAMS,
        cost_estimate=cost(14 * DH**3, 8 * DH * DH, 0),
        name="close_answer",
    )(place, *hbm(down), vmem(hidden), *hbm(attended), *[vmem(p) for p in parts])


def unpack_body(place_ref, *refs):
    out_ref = refs[4]
    core, yl, _ = seat(place_ref)
    for i, ref in enumerate(refs[:4]):
        head = 2 * (1 - yl if i // 2 else yl) + (1 - core if i % 2 else core)
        for which in range(4):

            @pl.when(head == which)
            def _():
                out_ref[:, which * DH : (which + 1) * DH] = ref[...]


def unpack(place, pieces):
    rows = pieces[0].shape[0]
    return pl.pallas_call(
        unpack_body,
        in_specs=[SM] + [VM] * 4,
        out_specs=VM,
        out_shape=shape((rows, 4 * DH)),
        compiler_params=PARAMS,
        cost_estimate=cost(0, 4 * rows * DH * 4),
        name="unpack",
    )(place, *[vmem(p) for p in pieces])


def swap(value, axis):
    return lax.all_to_all(
        value, axis, split_axis=0, concat_axis=0, tiled=True, axis_index_groups=[ORDERS[axis]]
    )


def step(fw_q, fw_k, fw_v, fw_lr, fast_gate, fast_up, fast_down, attn_q, attn_k, attn_v):
    place = lax.axis_index(CHIPS + QUAD).astype(jnp.int32).reshape(1)
    pair = [(0, 1), (1, 0)]
    weights = (fast_gate, fast_up, fast_down)
    rest = (fw_q, attn_q, attn_k, attn_v)
    own, send = pack_grad(place, fw_k, fw_v, fw_lr)
    send, *early = lax.optimization_barrier((send,) + weights)
    moved = lax.ppermute(send, "core", pair)
    picked, send = pick(place, early, rest)
    got = lax.ppermute(send, "core", pair)
    partial = grads(own, moved, picked)
    plane = lax.axis_size("plane")
    depth = lax.axis_size("z")
    part = swap(partial.reshape(plane, -1, DH), "plane")
    part = plane_sum(part)
    part = swap(part.reshape(depth, -1, DH), "z")
    last = last_rows(place, attn_k, attn_v, got)
    chips = lax.axis_size(CHIPS)
    halo = lax.ppermute(last, CHIPS, [(s, s + 1) for s in range(chips - 1)])
    part = sum_spread(part)
    part = swap(part, "z").reshape(-1, DH)
    cut = 2 * DH // PARTS
    first = jnp.broadcast_to(part[:cut], (plane, cut, DH))
    first = swap(first, "plane").reshape(PARTS, 2, -1, DH)
    second = part[cut:]
    parts = [second] + [
        lax.ppermute(second, "plane", move_along(*move)) for move in MOVES[1:]
    ]
    attended = attend(place, rest[1:], got, halo)
    hidden = open_answer(place, first, fast_gate, fast_up, fw_q, got)
    kept, to_core, to_chip, to_both = close_answer(place, parts, fast_down, hidden, attended)
    from_chip = lax.ppermute(to_chip, "yl", pair)
    from_both = lax.ppermute(to_both, QUAD, [(s, 3 - s) for s in range(4)])
    from_core = lax.ppermute(to_core, "core", pair)
    pieces = (kept, from_core, from_chip, from_both)
    return unpack(place, pieces)


def solution(mesh):
    fine = Mesh(mesh.devices.reshape(8, 8, 2, 2), ("z", "plane", "core", "yl"))
    ctx = ("z", "plane", "core")
    wide = P(ctx, "yl")
    weight = P("yl", None, None)
    in_specs = (wide, wide, wide, wide, weight, weight, weight, wide, wide, wide)
    out_specs = P(ctx + ("yl",), None)
    return jax.shard_map(step, mesh=fine, in_specs=in_specs, out_specs=out_specs, check_vma=False)
```

```python
import math

import jax
import jax.numpy as jnp
from jax import lax
from jax.experimental import pallas as pl
from jax.experimental.pallas import tpu as pltpu
from jax.sharding import Mesh, PartitionSpec as P

SWA_DH = 128
WINDOW = 128
NS_ITERS = 2
DH = 512
HALF = 256
PARTS = 8

linear_coef = 3.4445
square_coef = -4.775
quartic_coef = 2.0315
epsilon = 1e-06


CHIPS = ("z", "plane")
ORDERS = {"plane": [0, 5, 2, 7, 4, 1, 6, 3], "z": [7, 6, 5, 4, 3, 2, 1, 0]}
QUAD = ("core", "yl")

BF = jnp.bfloat16
F32 = jnp.float32
NN, NT, TN = ((1,), (0,)), ((1,), (1,)), ((0,), (0,))


def mat(left, right, dims):
    return lax.dot_general(left, right, (dims, ((), ())), preferred_element_type=F32)


def shape(dims, dtype=BF):
    return jax.ShapeDtypeStruct(dims, dtype)


def cost(flops, nbytes, trans=0):
    return pl.CostEstimate(flops=flops, bytes_accessed=nbytes, transcendentals=trans)


def vmem(value):
    return pltpu.with_memory_space_constraint(value, pltpu.VMEM)


def hbm(*values):
    return [pltpu.with_memory_space_constraint(v, pltpu.HBM) for v in values]


VM = pl.BlockSpec(memory_space=pltpu.VMEM)
SM = pl.BlockSpec(memory_space=pltpu.SMEM)
PARAMS = pltpu.CompilerParams(vmem_limit_bytes=24 * 1024 * 1024)


def on_chip(dims, dtype=BF):
    return pltpu.VMEM(dims, dtype)


HBM = pl.BlockSpec(memory_space=pltpu.HBM)


def seat(place_ref):
    place = place_ref[0]
    return (place >> 1) & 1, place & 1, place >> 2


def half(ref, which):
    return ref.at[:, pl.ds(pl.multiple_of(which * DH, DH), DH)]


def start_all(pairs, sems):
    copies = [pltpu.make_async_copy(a, b, sems.at[i]) for i, (a, b) in enumerate(pairs)]
    for copy in copies:
        copy.start()
    return copies


def wait_all(copies):
    for copy in copies:
        copy.wait()


def pack_grad_body(place_ref, k_ref, v_ref, lr_ref, own_ref, send_ref, value_ref, rate_ref, sems):
    core, _, _ = seat(place_ref)
    rows = k_ref.shape[0]
    sides = ((send_ref, 1 - core), (own_ref, core))
    pairs = [(half(v_ref, which), value_ref.at[i]) for i, (_, which) in enumerate(sides)]
    pairs += [(half(k_ref, which), ref.at[0]) for ref, which in sides]
    copies = start_all([(lr_ref, rate_ref)] + pairs, sems)
    copies[0].wait()
    for i, (ref, which) in enumerate(sides):
        copies[1 + i].wait()
        rates = jnp.where(which == 0, rate_ref[0:1, :], rate_ref[1:2, :])
        rates = jnp.broadcast_to(rates, (SWA_DH, rows)).T
        for j in range(0, DH, SWA_DH):
            value = value_ref[i, :, j : j + SWA_DH].astype(F32)
            ref[1, :, j : j + SWA_DH] = (-(rates * value)).astype(BF)
    wait_all(copies[3:])


def pack_grad(place, fw_k, fw_v, fw_lr):
    rows = fw_k.shape[0]
    return pl.pallas_call(
        pack_grad_body,
        in_specs=[SM, HBM, HBM, HBM],
        out_specs=[VM, VM],
        out_shape=[on_chip((2, rows, DH)), on_chip((2, rows, DH))],
        scratch_shapes=[
            pltpu.VMEM((2, rows, DH), BF),
            pltpu.VMEM((2, rows), F32),
            pltpu.SemaphoreType.DMA((5,)),
        ],
        compiler_params=PARAMS,
        cost_estimate=cost(rows * 1024, 8 * rows * 1024),
        name="pack_grad",
    )(place, *hbm(fw_k, fw_v, fw_lr.T))


def pick_body(place_ref, *refs):
    out_ref, send_ref, sems = refs[7:]
    core, _, _ = seat(place_ref)
    pairs = [(half(source, 1 - core), send_ref.at[i]) for i, source in enumerate(refs[3:7])]
    pairs += [(w.at[core], out_ref.at[i]) for i, w in enumerate(refs[:3])]
    wait_all(start_all(pairs, sems))


def pick(place, weights, arrays):
    rows = arrays[0].shape[0]
    return pl.pallas_call(
        pick_body,
        in_specs=[SM] + [HBM] * 7,
        out_specs=[VM, VM],
        out_shape=[on_chip((3, DH, DH)), on_chip((4, rows, DH))],
        scratch_shapes=[pltpu.SemaphoreType.DMA((7,))],
        compiler_params=PARAMS,
        cost_estimate=cost(0, 6 * DH * DH + 8 * rows * DH),
        name="pick",
    )(place, *hbm(*weights, *arrays))


def grads_body(own_ref, got_ref, weight_ref, out_ref):
    keys = jnp.concatenate([own_ref[0], got_ref[0]], axis=0)
    out_grad = jnp.concatenate([own_ref[1], got_ref[1]], axis=0)
    for h in range(DH // HALF):
        cols = slice(h * HALF, (h + 1) * HALF)
        pre_gate = mat(keys, weight_ref[0, :, cols], NN)
        pre_up = mat(keys, weight_ref[1, :, cols], NN)
        hidden_grad = mat(out_grad, weight_ref[2, cols, :], NT)
        sigmoid_gate = jax.nn.sigmoid(pre_gate)
        activated = pre_gate * sigmoid_gate
        hidden = (activated * pre_up).astype(BF)
        slope = sigmoid_gate * (1.0 + pre_gate * (1.0 - sigmoid_gate))
        gate_grad = (hidden_grad * pre_up * slope).astype(BF)
        up_grad = (hidden_grad * activated).astype(BF)
        out_ref[:, 0, :, cols] = mat(keys, gate_grad, TN).astype(BF).reshape(PARTS, -1, HALF)
        out_ref[:, 1, :, cols] = mat(keys, up_grad, TN).astype(BF).reshape(PARTS, -1, HALF)
        down = mat(hidden, out_grad, TN).astype(BF).reshape(PARTS // 2, -1, DH)
        out_ref[h * PARTS // 2 : (h + 1) * PARTS // 2, 2] = down


def grads(own, got, weights):
    tokens = 2 * own.shape[1]
    return pl.pallas_call(
        grads_body,
        in_specs=[VM] * 3,
        out_specs=VM,
        out_shape=on_chip((PARTS, 3, DH // PARTS, DH)),
        compiler_params=PARAMS,
        cost_estimate=cost(12 * tokens * DH * DH, 8 * DH * DH * 2, tokens * DH),
        name="grads",
    )(vmem(own), vmem(got), vmem(weights))


def add_up(in_ref, rows):
    total = in_ref[0, rows].astype(F32)
    for i in range(1, in_ref.shape[0]):
        total += in_ref[i, rows].astype(F32)
    return total.astype(BF)


def sum_body(in_ref, out_ref):
    for r in range(0, out_ref.shape[0], 16):
        rows = slice(r, r + 16)
        out_ref[rows] = add_up(in_ref, rows)


def plane_sum(parts):
    return pl.pallas_call(
        sum_body,
        in_specs=[VM],
        out_specs=VM,
        out_shape=shape(parts.shape[1:]),
        compiler_params=PARAMS,
        cost_estimate=cost(parts.size, 2 * parts.size),
        name="plane_sum",
    )(vmem(parts))


def tail_body(place_ref, k_ref, v_ref, got_ref, out_ref, sems):
    core, _, _ = seat(place_ref)
    tail = pl.ds(k_ref.shape[0] - WINDOW, WINDOW)
    kept = [(half(ref, 1).at[tail], out_ref.at[i]) for i, ref in enumerate((k_ref, v_ref))]
    other = [(got_ref.at[2 + i, tail], out_ref.at[i]) for i in range(2)]
    pl.when(core == 1)(lambda: wait_all(start_all(kept, sems)))
    pl.when(core != 1)(lambda: wait_all(start_all(other, sems)))


def last_rows(place, attn_k, attn_v, got):
    return pl.pallas_call(
        tail_body,
        in_specs=[SM, HBM, HBM, HBM],
        out_specs=VM,
        out_shape=on_chip((2, WINDOW, DH)),
        scratch_shapes=[pltpu.SemaphoreType.DMA((2,))],
        compiler_params=PARAMS,
        cost_estimate=cost(0, 8 * WINDOW * DH),
        name="tail",
    )(place, *hbm(attn_k, attn_v, got))


def sum_spread_body(in_ref, out_ref):
    total = add_up(in_ref, slice(None))
    for i in range(out_ref.shape[0]):
        out_ref[i] = total


def sum_spread(parts):
    return pl.pallas_call(
        sum_spread_body,
        in_specs=[VM],
        out_specs=VM,
        out_shape=shape(parts.shape),
        compiler_params=PARAMS,
        cost_estimate=cost(parts.size, 4 * parts.size),
        name="depth_sum",
    )(vmem(parts))


def spread_body(in_ref, out_ref, rest_ref, sems):
    cut = out_ref.shape[1]
    copies = start_all([(in_ref.at[:cut], out_ref.at[i]) for i in range(PARTS)], sems)
    rest_ref[...] = in_ref[cut:]
    wait_all(copies)


def spread(part):
    rows = part.shape[0]
    cut = 2 * rows // 3
    return pl.pallas_call(
        spread_body,
        in_specs=[VM],
        out_specs=[HBM, VM],
        out_shape=[pltpu.HBM((PARTS, cut, DH), BF), on_chip((rows - cut, DH))],
        scratch_shapes=[pltpu.SemaphoreType.DMA((PARTS,))],
        compiler_params=PARAMS,
        cost_estimate=cost(0, 2 * (PARTS + 1) * part.size),
        name="spread",
    )(vmem(part))


def attend_body(place_ref, own_q, own_k, own_v, got_ref, halo_ref, out_ref, *scratch):
    q_ref, k_ref, v_ref, result_ref, sems, out_sem = scratch
    core, _, chip = seat(place_ref)
    rows = own_q.shape[0]
    pairs = [(halo_ref.at[0], k_ref.at[:WINDOW]), (halo_ref.at[1], v_ref.at[:WINDOW])]
    own = [half(ref, core) for ref in (own_q, own_k, own_v)]
    for sources, which in ((own, core), ([got_ref.at[i] for i in (1, 2, 3)], 1 - core)):
        start = pl.multiple_of(which * rows, rows)
        pairs.append((sources[0], q_ref.at[pl.ds(start, rows)]))
        pairs.append((sources[1], k_ref.at[pl.ds(start + WINDOW, rows)]))
        pairs.append((sources[2], v_ref.at[pl.ds(start + WINDOW, rows)]))
    wait_all(start_all(pairs, sems))
    scale = 1.0 / math.sqrt(SWA_DH)
    row = lax.broadcasted_iota(jnp.int32, (WINDOW, 2 * WINDOW), 0)
    col = lax.broadcasted_iota(jnp.int32, (WINDOW, 2 * WINDOW), 1)
    inside = (col > row) & (col <= row + WINDOW)
    first = inside & ((col >= WINDOW) | (chip > 0))
    for b in range(2 * rows // WINDOW):
        seen = first if b == 0 else inside
        queries = slice(b * WINDOW, (b + 1) * WINDOW)
        window = slice(b * WINDOW, (b + 2) * WINDOW)
        for h in range(DH // SWA_DH):
            cols = slice(h * SWA_DH, (h + 1) * SWA_DH)
            scores = mat(q_ref[queries, cols], k_ref[window, cols], NT) * scale
            scores = jnp.where(seen, scores, -jnp.inf)
            exponent = jnp.exp(scores - jnp.max(scores, axis=-1, keepdims=True))
            total = jnp.sum(exponent, axis=-1, keepdims=True)
            probs = (exponent * (1.0 / total)).astype(BF)
            result_ref[queries, cols] = mat(probs, v_ref[window, cols], NN)
    copy = pltpu.make_async_copy(result_ref, out_ref, out_sem)
    copy.start()
    copy.wait()


def attend(place, own, got, halo):
    rows = got.shape[1]
    return pl.pallas_call(
        attend_body,
        in_specs=[SM, HBM, HBM, HBM, HBM, VM],
        out_specs=HBM,
        out_shape=pltpu.HBM((2 * rows, DH), F32),
        scratch_shapes=[
            pltpu.VMEM((2 * rows, DH), BF),
            pltpu.VMEM((2 * rows + WINDOW, DH), BF),
            pltpu.VMEM((2 * rows + WINDOW, DH), BF),
            pltpu.VMEM((2 * rows, DH), F32),
            pltpu.SemaphoreType.DMA((8,)),
            pltpu.SemaphoreType.DMA,
        ],
        compiler_params=PARAMS,
        cost_estimate=cost(2 * rows * 8 * WINDOW * DH, 12 * rows * DH, 4 * rows * DH),
        name="window_attention",
    )(place, *hbm(*own, got), vmem(halo))


def refresh(weight, update):
    initial = weight.astype(F32)
    stepped = initial - update.astype(F32)
    old_norm = jnp.sqrt(jnp.sum(initial * initial, axis=0, keepdims=True) + epsilon)
    new_norm = jnp.sqrt(jnp.sum(stepped * stepped, axis=0, keepdims=True) + epsilon)
    return (stepped * (old_norm / new_norm)).astype(BF)


MOVES = [(0, 0), (0, 1), (2, 1), (2, 0), (1, 1), (3, 1), (1, 0), (3, 0)]


def move_along(across, flip):
    def target(p):
        return ((p // 2 + across) % 4) * 2 + (p % 2 ^ flip)

    return [(p, target(p)) for p in range(PARTS)]


def orthogonal(gradients):
    iterates = []
    for gradient in gradients:
        gradient = gradient.reshape(DH, DH).astype(F32)
        norm_total = jnp.sum(gradient * gradient)
        iterates.append((gradient * (1.0 / jnp.sqrt(norm_total + epsilon))).astype(BF))
    for _ in range(NS_ITERS):
        grams = [mat(x, x, NT).astype(BF) for x in iterates]
        polys = [
            (square_coef * g.astype(F32) + quartic_coef * mat(g, g, NN)).astype(BF) for g in grams
        ]
        iterates = [
            (linear_coef * x.astype(F32) + mat(p, x, NN)).astype(BF)
            for p, x in zip(polys, iterates)
        ]
    return iterates


def open_body(place_ref, sum_ref, gate_ref, up_ref, own_ref, got_ref, out_ref, *scratch):
    weight_ref, query_ref, sems = scratch
    core, _, _ = seat(place_ref)
    rows = own_ref.shape[0]
    pairs = [(w.at[core], weight_ref.at[i]) for i, w in enumerate((gate_ref, up_ref))]
    for source, which in ((half(own_ref, core), core), (got_ref.at[0], 1 - core)):
        place = pl.ds(pl.multiple_of(which * rows, rows), rows)
        pairs.append((source, query_ref.at[place]))
    copies = start_all(pairs, sems)
    iterates = orthogonal([sum_ref[:, 0], sum_ref[:, 1]])
    wait_all(copies)
    gate, up = (refresh(weight_ref[i], x) for i, x in enumerate(iterates))
    query_gate = mat(query_ref[...], gate, NN)
    query_up = mat(query_ref[...], up, NN)
    out_ref[...] = (query_gate * jax.nn.sigmoid(query_gate) * query_up).astype(BF)


def open_answer(place, total, gate, up, own, got):
    rows = own.shape[0]
    return pl.pallas_call(
        open_body,
        in_specs=[SM, VM] + [HBM] * 4,
        out_specs=VM,
        out_shape=on_chip((2 * rows, DH)),
        scratch_shapes=[
            pltpu.VMEM((2, DH, DH), BF),
            pltpu.VMEM((2 * rows, DH), BF),
            pltpu.SemaphoreType.DMA((4,)),
        ],
        compiler_params=PARAMS,
        cost_estimate=cost(28 * DH**3, 12 * DH * DH, rows * DH),
        name="open_answer",
    )(place, vmem(total), *hbm(gate, up, own, got))


def close_body(place_ref, down_ref, hidden_ref, att_ref, *rest):
    part_refs, out_refs = rest[:PARTS], rest[PARTS : PARTS + 4]
    all_ref, sum_ref, weight_ref, attended_ref, sems = rest[PARTS + 4 :]
    core, yl, chip = seat(place_ref)
    copies = start_all([(down_ref.at[core], weight_ref), (att_ref, attended_ref)], sems)
    x, yh = (chip >> 1) & 3, chip & 1
    for ref, (across, flip) in zip(part_refs, MOVES):
        source = ((x - across) & 3) * 2 + (yh ^ flip)
        sum_ref[source ^ ((source & 1) * 4)] = ref[...]
    (iterate,) = orthogonal([sum_ref[...]])
    wait_all(copies)
    down = refresh(weight_ref[...], iterate)
    memory = mat(hidden_ref[...], down, NN).astype(BF)
    all_ref[...] = (memory.astype(F32) + attended_ref[...]).astype(BF)
    block = out_refs[0].shape[0]
    for i, ref in enumerate(out_refs):
        to_core = 1 - core if i % 2 else core
        to_yl = 1 - yl if i // 2 else yl
        ref[...] = all_ref[pl.ds(pl.multiple_of((to_core * 2 + to_yl) * block, block), block)]


def close_answer(place, parts, down, hidden, attended):
    rows = hidden.shape[0]
    return pl.pallas_call(
        close_body,
        in_specs=[SM, HBM, VM, HBM] + [VM] * PARTS,
        out_specs=[VM] * 4,
        out_shape=[on_chip((rows // 4, DH))] * 4,
        scratch_shapes=[
            pltpu.VMEM((rows, DH), BF),
            pltpu.VMEM((PARTS, DH // PARTS, DH), BF),
            pltpu.VMEM((DH, DH), BF),
            pltpu.VMEM((rows, DH), F32),
            pltpu.SemaphoreType.DMA((2,)),
        ],
        compiler_params=PARAMS,
        cost_estimate=cost(14 * DH**3, 8 * DH * DH, 0),
        name="close_answer",
    )(place, *hbm(down), vmem(hidden), *hbm(attended), *[vmem(p) for p in parts])


def unpack_body(place_ref, *refs):
    out_ref = refs[4]
    core, yl, _ = seat(place_ref)
    for i, ref in enumerate(refs[:4]):
        head = 2 * (1 - yl if i // 2 else yl) + (1 - core if i % 2 else core)
        for which in range(4):

            @pl.when(head == which)
            def _():
                out_ref[:, which * DH : (which + 1) * DH] = ref[...]


def unpack(place, pieces):
    rows = pieces[0].shape[0]
    return pl.pallas_call(
        unpack_body,
        in_specs=[SM] + [VM] * 4,
        out_specs=VM,
        out_shape=shape((rows, 4 * DH)),
        compiler_params=PARAMS,
        cost_estimate=cost(0, 4 * rows * DH * 4),
        name="unpack",
    )(place, *[vmem(p) for p in pieces])


def swap(value, axis):
    return lax.all_to_all(
        value, axis, split_axis=0, concat_axis=0, tiled=True, axis_index_groups=[ORDERS[axis]]
    )


def step(fw_q, fw_k, fw_v, fw_lr, fast_gate, fast_up, fast_down, attn_q, attn_k, attn_v):
    place = lax.axis_index(CHIPS + QUAD).astype(jnp.int32).reshape(1)
    pair = [(0, 1), (1, 0)]
    weights = (fast_gate, fast_up, fast_down)
    rest = (fw_q, attn_q, attn_k, attn_v)
    own, send = pack_grad(place, fw_k, fw_v, fw_lr)
    send, *early = lax.optimization_barrier((send,) + weights)
    moved = lax.ppermute(send, "core", pair)
    picked, send = pick(place, early, rest)
    got = lax.ppermute(send, "core", pair)
    partial = grads(own, moved, picked)
    plane = lax.axis_size("plane")
    depth = lax.axis_size("z")
    part = swap(partial.reshape(plane, -1, DH), "plane")
    part = plane_sum(part)
    part = swap(part.reshape(depth, -1, DH), "z")
    last = last_rows(place, attn_k, attn_v, got)
    chips = lax.axis_size(CHIPS)
    halo = lax.ppermute(last, CHIPS, [(s, s + 1) for s in range(chips - 1)])
    part = sum_spread(part)
    part = swap(part, "z").reshape(-1, DH)
    first, second = spread(part)
    first = swap(first, "plane").reshape(PARTS, 2, -1, DH)
    parts = [second] + [
        lax.ppermute(second, "plane", move_along(*move)) for move in MOVES[1:]
    ]
    attended = attend(place, rest[1:], got, halo)
    hidden = open_answer(place, first, fast_gate, fast_up, fw_q, got)
    kept, to_core, to_chip, to_both = close_answer(place, parts, fast_down, hidden, attended)
    from_chip = lax.ppermute(to_chip, "yl", pair)
    from_both = lax.ppermute(to_both, QUAD, [(s, 3 - s) for s in range(4)])
    from_core = lax.ppermute(to_core, "core", pair)
    pieces = (kept, from_core, from_chip, from_both)
    return unpack(place, pieces)


def solution(mesh):
    fine = Mesh(mesh.devices.reshape(8, 8, 2, 2), ("z", "plane", "core", "yl"))
    ctx = ("z", "plane", "core")
    wide = P(ctx, "yl")
    weight = P("yl", None, None)
    in_specs = (wide, wide, wide, wide, weight, weight, weight, wide, wide, wide)
    out_specs = P(ctx + ("yl",), None)
    return jax.shard_map(step, mesh=fine, in_specs=in_specs, out_specs=out_specs, check_vma=False)
```
